32 devices in a mesh: section: 2 (over x), dp: 16 (over z, y, core).
Axes of the slice: x: 2, y: 2, z: 4, core: 2. Of those that a mesh axis runs over, the one named last changes fastest.
Arguments:
- embeds: bfloat16 [3072, 3584], P('dp'), may hold values from -16 to 16
- cotangent: bfloat16 [3072, 3584], P('dp'), may hold values from -1 to 1
- adapter_a: bfloat16 [2, 7168, 128], P('section', 'dp'), may hold values from -0.0625 to 0.0625
- adapter_b: bfloat16 [2, 128, 3584], P('section', None, 'dp'), may hold values from -0.5 to 0.5
- norm_gains: float32 [2, 7168], replicated, may hold values from 0.5 to 1.5
Outputs:
- grad_a: float32 [2, 7168, 128], P('section', 'dp')
- grad_b: float32 [2, 128, 3584], P('section')
- grad_gain: float32 [2, 7168], P(None, 'dp')
- grad_embed: bfloat16 [3072, 3584], P('dp', 'section')
The draws below stay inside these ranges and needn't reach their ends.
All inputs are finite; a program needn't handle non-finite values.
Results may differ from the reference program's by a relative error of at most 0.023.
Values may be sent and summed in bfloat16 or wider, within the bound.
No kernel may reach another device: no remote copies, remote signals or barrier semaphores. Data moves between devices by JAX's collectives and lax.ppermute only.
A program may use at most 64 MiB of HBM per device.

```python
import math
import jax
import jax.numpy as jnp
from jax import lax

D = 3584
R = 128
CAT = 7168
TOKENS = 3072
SECTIONS = 2


def draw_embeds(key, part):
    row_key, col_key, base_key = jax.random.split(key, 3)
    row_scale = jnp.exp(jax.random.uniform(row_key, (TOKENS, 1), jnp.float32, math.log(0.3), math.log(3.0)))
    col_scale = jnp.exp(jax.random.uniform(col_key, (1, D), jnp.float32, math.log(0.3), math.log(3.0)))
    base_draw = jax.random.normal(base_key, (TOKENS, D), jnp.float32)
    return jnp.clip(base_draw * row_scale * col_scale, -16.0, 16.0).astype(jnp.bfloat16)


def strengthened(result, rng, source, target, shards_of, factor):
    owner, partner = [(jnp.arange(result.shape[dim]) // (result.shape[dim] // shards_of)).reshape([-1 if axis == dim else 1 for axis in range(result.ndim)]) for dim in (source, target)]
    chosen = jax.random.permutation(rng, shards_of)[partner]
    strong = (owner == chosen) | (owner == (partner + shards_of // 2) % shards_of)
    return jnp.where(strong, factor * result, result)


def shard_levels(stream_key, extent, cuts, smallest, largest):
    gain = 1.0
    for dim, blocks in cuts:
        draws = jax.random.uniform(jax.random.fold_in(jax.random.fold_in(stream_key, 6), dim), (blocks,), jnp.float32, smallest / len(cuts), largest / len(cuts))
        gain = gain * jnp.repeat(jnp.exp(draws), extent[dim] // blocks).reshape((-1,) + (1,) * (len(extent) - 1 - dim))
    return gain


def noise(own_key, dims, scale, limit, pieces=(), kind=jnp.bfloat16):
    result = scale * jax.random.normal(own_key, dims, jnp.float32)
    if pieces:
        result = result * shard_levels(own_key, dims, pieces, -0.22, 0.18)
    return jnp.clip(result, -limit, limit).astype(kind)


def heavy_noise(own_key, dims, spread, reach, cuts, heavy, held_as=jnp.bfloat16):
    result = spread * jax.random.normal(own_key, dims, jnp.float32)
    if cuts:
        result = result * shard_levels(own_key, dims, cuts, -0.22, 0.18)
    return jnp.clip(strengthened(result, jax.random.fold_in(own_key, 3), *heavy), -reach, reach).astype(held_as)


def setup_inputs(seed: int = 0) -> dict:
    splits = jax.random.split(jax.random.key(seed), 6)
    embeds = draw_embeds(jax.random.fold_in(splits[5], 71), 0)
    cotangent = heavy_noise(splits[1], (TOKENS, D), 0.125, 1.0, ((0, 16),), (0, 1, 16, 2.0))
    adapter_a = noise(splits[2], (SECTIONS, CAT, R), CAT ** -0.5, 0.0625, ((0, 2), (1, 16)))
    adapter_b = noise(splits[3], (SECTIONS, R, D), R ** -0.5, 0.5, ((0, 2), (2, 16)))
    norm_gains = jnp.clip(1.0 + 0.1 * jax.random.normal(splits[4], (2, CAT), jnp.float32), 0.5, 1.5)
    return dict(embeds=embeds, cotangent=cotangent, adapter_a=adapter_a, adapter_b=adapter_b, norm_gains=norm_gains)


epsilon = 1e-05

def normalize(hidden, embeds, gain_row):
    joined = jnp.concatenate([hidden.astype(jnp.float32), embeds.astype(jnp.float32)], axis=1)
    inv_rms = lax.rsqrt(lax.optimization_barrier(jnp.mean(joined * joined, axis=1, keepdims=True)) + epsilon)
    normed = joined * inv_rms
    lowered = (normed * gain_row[None, :]).astype(jnp.bfloat16)
    return (normed, inv_rms, lowered)

def reference(embeds, cotangent, adapter_a, adapter_b, norm_gains):
    hidden = embeds
    inputs = []
    for section in range(SECTIONS):
        normed, inv_rms, lowered = normalize(hidden, embeds, norm_gains[section % 2])
        reduced = jnp.dot(lowered, adapter_a[section], preferred_element_type=jnp.float32).astype(jnp.bfloat16)
        inputs.append(hidden)
        hidden = (hidden.astype(jnp.float32) + jnp.dot(reduced, adapter_b[section], preferred_element_type=jnp.float32)).astype(jnp.bfloat16)
    back = cotangent
    grads_a = []
    grads_b = []
    gain_total = jnp.zeros((2, CAT), jnp.float32)
    embed_total = jnp.zeros((TOKENS, D), jnp.float32)
    for section in reversed(range(SECTIONS)):
        gain_row = norm_gains[section % 2]
        normed, inv_rms, lowered = normalize(inputs[section], embeds, gain_row)
        reduced = jnp.dot(lowered, adapter_a[section], preferred_element_type=jnp.float32).astype(jnp.bfloat16)
        up_grad = jnp.dot(back, adapter_b[section].T, preferred_element_type=jnp.float32).astype(jnp.bfloat16)
        grads_b.append(jnp.dot(reduced.T, back, preferred_element_type=jnp.float32))
        grad_lowered = jnp.dot(up_grad, adapter_a[section].T, preferred_element_type=jnp.float32)
        grads_a.append(jnp.dot(lowered.T, up_grad, preferred_element_type=jnp.float32))
        gain_part = lax.optimization_barrier(jnp.sum(grad_lowered * normed, axis=0)).astype(jnp.bfloat16)
        gain_part = lax.optimization_barrier(gain_part)
        scaled = grad_lowered * gain_row[None, :]
        grad_joined = inv_rms * (scaled - normed * lax.optimization_barrier(jnp.mean(scaled * normed, axis=1, keepdims=True)))
        back = (back.astype(jnp.float32) + grad_joined[:, :D]).astype(jnp.bfloat16)
        embed_tail = grad_joined[:, D:]
        if section == 0:
            embed_tail = embed_tail + back.astype(jnp.float32)
        embed_part = lax.optimization_barrier(embed_tail.astype(jnp.bfloat16))
        embed_total = embed_total + embed_part.astype(jnp.float32)
        gain_total = gain_total.at[section % 2].add(gain_part.astype(jnp.float32))
    grad_a = jnp.stack(grads_a[::-1])
    grad_b = jnp.stack(grads_b[::-1])
    return (grad_a, grad_b, gain_total, embed_total.astype(jnp.bfloat16))
```

```python
import functools

import jax
import jax.numpy as jnp
from jax import lax
from jax.experimental import pallas as pl
from jax.experimental.pallas import tpu as pltpu
from jax.sharding import PartitionSpec as P

epsilon = 1e-05

F32 = jnp.float32
BF16 = jnp.bfloat16

CORE, Y, ZN, ZF = 1, 2, 4, 8
CHIPS = (0, ZN, ZF, Y, ZN | ZF, ZN | Y, ZF | Y, ZN | ZF | Y)


def dot(left, right, left_dim=1, right_dim=0):
    return lax.dot_general(
        left, right, (((left_dim,), (right_dim,)), ((), ())), preferred_element_type=F32
    )


def swap(block, mask):
    count = lax.axis_size("dp")
    return lax.ppermute(block, "dp", [(i, i ^ mask) for i in range(count)])


def cross(block):
    return lax.ppermute(block, "section", [(0, 1), (1, 0)])


def transpose_sections(block, mask):
    count = lax.axis_size("dp")
    route = []
    for section in range(2):
        for index in range(count):
            mine = section * count + index
            other = (1 - section) * count + (index ^ mask)
            route.append((mine, mine if bool(index & mask) == bool(section) else other))
    return lax.ppermute(block, ("section", "dp"), route)


def gather_chips(own):
    near = swap(own, ZN)
    far = swap(own, ZF)
    side = swap(own, Y)
    both = swap(near, ZF)
    side_two = swap(jnp.stack([near, far]), Y)
    side_both = swap(both, Y)
    early = jnp.stack([own, near, far, side])
    late = jnp.concatenate([jnp.stack([both]), side_two, jnp.stack([side_both])])
    return early, late


def gather_plane(own):
    early, late = gather_chips(own)
    return early, late, swap(early, CORE), swap(late, CORE)


def add(left, right):
    return (left.astype(F32) + right.astype(F32)).astype(BF16)


def reduce_plane(keep, send):
    total = add(keep, swap(send, CORE))
    both = add(total[4], swap(total[7], Y))
    pair = add(total[1:3], swap(total[5:7], Y))
    near = add(pair[0], swap(both, ZF))
    far = pair[1]
    side = swap(total[3], Y)
    return add(
        add(total[0], side).astype(F32) + swap(far, ZF).astype(F32), swap(near, ZN)
    )


def place_kernel(rows_a, ids, e_ref, c_ref, early, late, early2, late2, pay_ref, a_ref, b_ref, sems):
    index = ids[1]
    copies = []
    for core, (first, second) in enumerate(((early, late), (early2, late2))):
        for k, chip in enumerate(CHIPS):
            holder = jnp.bitwise_xor(index, chip | core)
            source = first.at[k] if k < 4 else second.at[k - 4]
            slot = 2 * (8 * core + k)
            copies.append(
                pltpu.make_async_copy(
                    source.at[pl.ds(0, rows_a)],
                    a_ref.at[lax.div(holder, 4), lax.rem(holder, 4)],
                    sems.at[slot],
                )
            )
            copies.append(
                pltpu.make_async_copy(
                    source.at[pl.ds(rows_a, rows_a // 2)],
                    b_ref.at[lax.div(holder, 8), lax.rem(holder, 8)],
                    sems.at[slot + 1],
                )
            )
    for copy in copies:
        copy.start()
    for copy in copies:
        copy.wait()
    cols = 4 * rows_a
    rank = a_ref.shape[3]
    rows = e_ref.shape[0]
    p0, p1, q0, q1 = (a_ref[k].reshape(cols, rank) for k in range(4))
    b0, b1 = (b_ref[k].reshape(cols, rank) for k in range(2))
    w0 = (p0.astype(F32) + q0.astype(F32)).astype(BF16)
    w1 = (p1.astype(F32) + q1.astype(F32)).astype(BF16)
    e = e_ref[...]
    c = c_ref[...]
    for k, value in enumerate((dot(e, w0), dot(e, w1), dot(e, b0), dot(c, b0), dot(c, b1))):
        pay_ref[pl.ds(k * rows, rows), :] = value.astype(BF16)
    base = 5 * rows
    mixed = dot(b0, p1, 0, 0)
    square = dot(b0, b0, 0, 0)
    high = square.astype(BF16)
    pay_ref[pl.ds(base, rank), :] = mixed.astype(BF16)
    pay_ref[pl.ds(base + rank, rank), :] = high
    pay_ref[pl.ds(base + 2 * rank, rank), :] = (square - high.astype(F32)).astype(BF16)


def rows_kernel(
    width, ids, e_ref, c_ref, mine, other, norm_ref, a_ref, b_ref,
    keep_ref, send_ref, back_ref, v_ref, coef_ref, apan, hpan,
):
    index = ids[1]
    rows, cols = e_ref.shape
    rank = a_ref.shape[3]
    blk = a_ref.shape[2]

    def total(start, size):
        part = pl.ds(start, size)
        return mine[part, :].astype(F32) + other[part, :].astype(F32)

    a0, a1, e0, y0, y1 = (total(k * rows, rows) for k in range(5))
    base = 5 * rows
    mixed = total(base, rank).astype(BF16)
    square = total(base + rank, rank) + total(base + 2 * rank, rank)
    high = square.astype(BF16)
    low = (square - high.astype(F32)).astype(BF16)
    norm = norm_ref[...]
    scale = 1.0 / (2 * width)

    inv0 = lax.rsqrt(2.0 * norm * scale + epsilon)
    r0 = (inv0 * a0).astype(BF16)
    r0f = r0.astype(F32)
    r0s = dot(r0, high) + dot(r0, low)
    full = 2.0 * norm + jnp.sum(r0f * (2.0 * e0 + r0s), axis=1, keepdims=True)
    inv1 = lax.rsqrt(jnp.maximum(full, norm) * scale + epsilon)
    r1f = inv1 * (a1 + dot(r0, mixed))
    r1 = r1f.astype(BF16)
    m1 = jnp.sum(y1 * r1f, axis=1, keepdims=True) * scale
    c1 = inv1 * inv1 * m1
    v1 = (inv1 * y1).astype(BF16)
    u0 = y0 + dot(v1, mixed, 1, 1) - c1 * (e0 + r0s)
    m0 = jnp.sum(u0 * r0f, axis=1, keepdims=True) * scale
    c0 = inv0 * inv0 * m0
    v0 = (inv0 * u0).astype(BF16)

    e = e_ref[...]
    c = c_ref[...]
    b0 = b_ref[0].reshape(cols, rank)
    p1 = a_ref[1].reshape(cols, rank)
    h1f = e.astype(F32) + dot(r0, b0, 1, 1)
    backf = c.astype(F32) + dot(v1, p1, 1, 1) - c1 * h1f
    h1 = h1f.astype(BF16)
    back = backf.astype(BF16)
    back_ref[...] = back
    v_ref[0] = v0
    v_ref[1] = v1
    coef_ref[...] = jnp.broadcast_to(2.0 * c0 + c1, coef_ref.shape)

    g0 = dot(e, v0, 0, 0).astype(BF16).reshape(4, blk, rank)
    apan[0] = g0
    apan[2] = g0
    apan[1] = dot(h1, v1, 0, 0).astype(BF16).reshape(4, blk, rank)
    apan[3] = dot(e, v1, 0, 0).astype(BF16).reshape(4, blk, rank)
    hpan[0] = dot(back, r0, 0, 0).astype(BF16).reshape(8, blk // 2, rank)
    hpan[1] = dot(c, r1, 0, 0).astype(BF16).reshape(8, blk // 2, rank)
    for core, out in enumerate((keep_ref, send_ref)):
        for k, chip in enumerate(CHIPS):
            holder = jnp.bitwise_xor(index, chip | core)
            out[k, pl.ds(0, blk), :] = apan[lax.div(holder, 4), lax.rem(holder, 4)]
            out[k, pl.ds(blk, blk // 2), :] = hpan[lax.div(holder, 8), lax.rem(holder, 8)]


def embed_kernel(ids, e_ref, back_ref, v_ref, coef_ref, a_ref, out_ref):
    rows, cols = e_ref.shape
    rank = a_ref.shape[3]
    w0 = (a_ref[0].astype(F32) + a_ref[2].astype(F32)).astype(BF16).reshape(cols, rank)
    q1 = a_ref[3].reshape(cols, rank)
    out_ref[...] = (
        back_ref[...].astype(F32)
        + dot(v_ref[0], w0, 1, 1)
        + dot(v_ref[1], q1, 1, 1)
        - coef_ref[:, 0:1] * e_ref[...].astype(F32)
    ).astype(BF16)


def up_kernel(ids, early, late, early2, late2, out_ref, natural, sems):
    index = ids[1]
    copies = []
    for core, (first, second) in enumerate(((early, late), (early2, late2))):
        for k, chip in enumerate(CHIPS):
            holder = jnp.bitwise_xor(index, chip | core)
            source = first.at[k] if k < 4 else second.at[k - 4]
            copies.append(
                pltpu.make_async_copy(source, natural.at[holder], sems.at[8 * core + k])
            )
    for copy in copies:
        copy.start()
    for copy in copies:
        copy.wait()
    blocks, size, rank = natural.shape
    out_ref[...] = natural[...].reshape(blocks * size, rank).astype(F32).T


def spec(shape, index=None):
    if index is None:
        return pl.BlockSpec(shape, lambda i, ids: (0,) * len(shape))
    return pl.BlockSpec(shape, index)


ANY = pl.BlockSpec(memory_space=pl.ANY)
LIMIT = pltpu.CompilerParams(vmem_limit_bytes=56 * 1024 * 1024)


def call(kernel, ids, operands, in_specs, outs, scratch=()):
    return pl.pallas_call(
        kernel,
        out_shape=[jax.ShapeDtypeStruct(shape, dtype) for shape, dtype in outs],
        grid_spec=pltpu.PrefetchScalarGridSpec(
            num_scalar_prefetch=1,
            grid=(1,),
            in_specs=in_specs,
            out_specs=[spec(shape) for shape, _ in outs],
            scratch_shapes=list(scratch),
        ),
        compiler_params=LIMIT,
    )(ids, *operands)


def paired(embeds, cotangent, adapter_a, adapter_b, norm_gains):
    section = lax.axis_index("section")
    index = lax.axis_index("dp")
    ids = jnp.stack([section, index]).astype(jnp.int32)
    rows, width = embeds.shape
    cols = width // 2
    down = adapter_a[0]
    blk, rank = down.shape
    half = blk // 2
    gain_row = lax.dynamic_index_in_dim(norm_gains, section, 0, keepdims=False)
    gain = lax.dynamic_slice_in_dim(gain_row, index * blk, blk, 0)[:, None]
    scaled = (down.astype(F32) * gain).astype(BF16)

    own = jnp.concatenate(
        [transpose_sections(scaled, ZN), transpose_sections(adapter_b[0].T, ZF)]
    )
    parts = gather_plane(own)
    norm = jnp.sum(jnp.square(embeds.astype(F32)), axis=1, keepdims=True)

    column = pl.BlockSpec((rows, cols), lambda i, ids: (0, ids[0]))
    pay = 5 * rows + 3 * rank
    payload, a_all, b_all = call(
        functools.partial(place_kernel, blk),
        ids,
        (embeds, cotangent, *parts),
        [column, column, ANY, ANY, ANY, ANY],
        [((pay, rank), BF16), ((4, 4, blk, rank), BF16), ((2, 8, half, rank), BF16)],
        [pltpu.SemaphoreType.DMA((32,))],
    )
    other = cross(payload)
    keep, send, back, vees, coef = call(
        functools.partial(rows_kernel, width),
        ids,
        (embeds, cotangent, payload, other, norm, a_all, b_all),
        [
            column, column, spec((pay, rank)), spec((pay, rank)), spec((rows, 1)),
            spec((4, 4, blk, rank)), spec((2, 8, half, rank)),
        ],
        [
            ((8, blk + half, rank), BF16), ((8, blk + half, rank), BF16),
            ((rows, cols), BF16), ((2, rows, rank), BF16), ((rows, rank), F32),
        ],
        [pltpu.VMEM((4, 4, blk, rank), BF16), pltpu.VMEM((2, 8, half, rank), BF16)],
    )
    (embed_cols,) = call(
        embed_kernel,
        ids,
        (embeds, back, vees, coef, a_all),
        [
            column, spec((rows, cols)), spec((2, rows, rank)), spec((rows, rank)),
            spec((4, 4, blk, rank)),
        ],
        [((rows, cols), BF16)],
    )
    sums = reduce_plane(keep, send)
    up_own = transpose_sections(sums[blk:], ZF)
    up_parts = gather_plane(up_own)
    (grad_b,) = call(
        up_kernel,
        ids,
        up_parts,
        [ANY] * 4,
        [((rank, width), F32)],
        [pltpu.VMEM((16, half, rank), BF16), pltpu.SemaphoreType.DMA((16,))],
    )
    outer = transpose_sections(sums[:blk], ZN).astype(F32)
    gain_part = jnp.sum(outer * down.astype(F32), axis=1)
    gain_other = cross(gain_part)
    first = jnp.where(section == 0, gain_part, gain_other)
    second = jnp.where(section == 0, gain_other, gain_part)
    return ((gain * outer)[None], grad_b[None], jnp.stack([first, second]), embed_cols)


def general(embeds, cotangent, adapter_a, adapter_b, norm_gains):
    sections = lax.axis_size("section")
    section = lax.axis_index("section")
    index = lax.axis_index("dp")
    rows, width = embeds.shape
    cols = width // sections
    down = adapter_a[0]
    blk, rank = down.shape
    gain_row = lax.dynamic_index_in_dim(norm_gains, section % 2, 0, keepdims=False)
    gain = lax.dynamic_slice_in_dim(gain_row, index * blk, blk, 0)[:, None]
    scaled = (down.astype(F32) * gain).astype(BF16)
    down_all = lax.all_gather(lax.all_gather(scaled, "dp", axis=0, tiled=True), "section")
    up_all = lax.all_gather(lax.all_gather(adapter_b[0].T, "dp", axis=0, tiled=True), "section")
    start = section * cols
    tops = lax.dynamic_slice_in_dim(down_all, start, cols, 1)
    bottoms = lax.dynamic_slice_in_dim(down_all, width + start, cols, 1)
    ups = lax.dynamic_slice_in_dim(up_all, start, cols, 1)
    e = lax.dynamic_slice_in_dim(embeds, start, cols, 1)
    c = lax.dynamic_slice_in_dim(cotangent, start, cols, 1)
    norm = jnp.sum(jnp.square(embeds.astype(F32)), axis=1, keepdims=True)

    def project(left, right):
        return lax.dot_general(right, left, (((1,), (1,)), ((), ())), preferred_element_type=F32)

    def pairs(left, right):
        return jnp.einsum("tcr,ucq->turq", left, right, preferred_element_type=F32)

    lows, ups_e, ups_c, mixed, square = lax.psum(
        (
            project(e, tops) + project(e, bottoms),
            project(e, ups),
            project(c, ups),
            pairs(ups, tops),
            pairs(ups, ups),
        ),
        "section",
    )
    lows, ups_e, ups_c = (jnp.swapaxes(value, 1, 2) for value in (lows, ups_e, ups_c))
    scale = 1.0 / (2 * width)

    def exact(left, right):
        return jnp.dot(left, right, precision=lax.Precision.HIGHEST)

    reds, invs, spans = [], [], []
    for s in range(sections):
        full = 2.0 * norm
        low = lows[s]
        for t in range(s):
            red = reds[t].astype(F32)
            low = low + exact(red, mixed[t, s])
            full = full + jnp.sum(red * (2.0 * ups_e[t]), axis=1, keepdims=True)
            for q in range(s):
                other = exact(reds[q].astype(F32), square[q, t])
                full = full + jnp.sum(red * other, axis=1, keepdims=True)
        inv = lax.rsqrt(jnp.maximum(full, norm) * scale + epsilon)
        invs.append(inv)
        spans.append(inv * low)
        reds.append((inv * low).astype(BF16))
    vees, coefs = [None] * sections, [None] * sections
    for s in reversed(range(sections)):
        grad = ups_c[s]
        for t in range(s + 1, sections):
            hidden = ups_e[s]
            for q in range(t):
                hidden = hidden + exact(reds[q].astype(F32), square[q, s])
            grad = grad + exact(vees[t].astype(F32), mixed[s, t].T) - coefs[t] * hidden
        mean = jnp.sum(grad * spans[s], axis=1, keepdims=True) * scale
        coefs[s] = invs[s] * invs[s] * mean
        vees[s] = (invs[s] * grad).astype(BF16)
    hiddens = [e.astype(F32)]
    for s in range(sections - 1):
        hiddens.append(hiddens[s] + dot(reds[s], ups[s], 1, 1))
    back = c.astype(F32)
    embed_cols = jnp.zeros_like(back)
    terms = [None] * sections
    for s in reversed(range(sections)):
        h = hiddens[s].astype(BF16)
        terms[s] = jnp.stack(
            [
                dot(h, vees[s], 0, 0),
                dot(e, vees[s], 0, 0),
                dot(back.astype(BF16), reds[s], 0, 0),
            ]
        )
        embed_cols = embed_cols + dot(vees[s], bottoms[s], 1, 1) - coefs[s] * e.astype(F32)
        back = back + dot(vees[s], tops[s], 1, 1) - coefs[s] * hiddens[s]
    embed_cols = (embed_cols + back).astype(BF16)
    sums = lax.psum(jnp.stack(terms), "dp")
    mine = lax.all_to_all(sums, "section", 0, 2, tiled=True)[0]
    outer = lax.dynamic_slice_in_dim(mine[:2].reshape(2 * width, rank), index * blk, blk, 0)
    part = jnp.sum(outer * down.astype(F32), axis=1)
    parity = section % 2
    gain_pair = jnp.stack([jnp.where(parity == 0, part, 0.0), jnp.where(parity == 1, part, 0.0)])
    return ((gain * outer)[None], mine[2].T[None], lax.psum(gain_pair, "section"), embed_cols)


def solution(mesh):
    in_specs = (
        P("dp", None),
        P("dp", None),
        P("section", "dp", None),
        P("section", None, "dp"),
        P(),
    )
    out_specs = (
        P("section", "dp", None),
        P("section", None, None),
        P(None, "dp"),
        P("dp", "section"),
    )
    body = paired if mesh.shape["section"] == 2 and mesh.shape["dp"] == 16 else general
    return jax.shard_map(
        body, mesh=mesh, in_specs=in_specs, out_specs=out_specs, check_vma=False
    )
```

```python
import jax
import jax.numpy as jnp
from jax import lax
from jax.experimental import pallas as pl
from jax.experimental.pallas import tpu as pltpu
from jax.sharding import PartitionSpec as P

epsilon = 1e-05

F32 = jnp.float32
BF16 = jnp.bfloat16

CORE, Y, NEAR, FAR = 1, 2, 4, 8


def dot(left, right, left_dim=1, right_dim=0):
    return lax.dot_general(
        left, right, (((left_dim,), (right_dim,)), ((), ())), preferred_element_type=F32
    )


def swap(block, mask):
    count = lax.axis_size("dp")
    return lax.ppermute(block, "dp", [(i, i ^ mask) for i in range(count)])


def cross(block, mask=0):
    count = lax.axis_size("dp")
    route = [(i, (i + count) % (2 * count) ^ mask) for i in range(2 * count)]
    return lax.ppermute(block, ("section", "dp"), route)


def trade(block, mask, step):
    count = lax.axis_size("dp")
    route = []
    for section in range(2):
        for index in range(count):
            to_section, to_bit = step(section, int(bool(index & mask)))
            target = to_section * count + ((index & ~mask) | (mask if to_bit else 0))
            route.append((section * count + index, target))
    return lax.ppermute(block, ("section", "dp"), route)


def turned(s, b):
    return (b, s)


def spread(s, b):
    return (s, 1 - b) if s == b else (1 - s, b)


def joined(s, b):
    return (1 - s, b) if s == b else (s, 1 - b)


def add(left, right):
    return (left.astype(F32) + right.astype(F32)).astype(BF16)


def gather_up(pair):
    early = jnp.stack([pair, swap(pair, NEAR), swap(pair, Y), swap(pair, NEAR | Y)])
    return early, swap(early, CORE)


UP_MASKS = (0, NEAR, Y, NEAR | Y)


def gather_down(pair):
    far = swap(pair, FAR)
    early = jnp.stack([pair, swap(pair, Y)])
    late = jnp.stack([far, swap(far, Y)])
    return early, late, swap(early, CORE), swap(late, CORE)


DOWN_MASKS = (0, Y, FAR, FAR | Y, CORE, CORE | Y, CORE | FAR, CORE | FAR | Y)


def up_kernel(ids, e_ref, c_ref, early, late, pay_ref, b_ref):
    section, index = ids[0], ids[1]
    bit = lax.rem(lax.div(index, FAR), 2)
    for core, blocks in enumerate((early, late)):
        for k, mask in enumerate(UP_MASKS):
            place = lax.rem(jnp.bitwise_xor(index, mask | core), 8)
            for j in range(2):
                b_ref[jnp.bitwise_xor(bit, j), place] = blocks[k, j]
    cols = b_ref.shape[1] * b_ref.shape[2]
    rank = b_ref.shape[3]
    rows = e_ref.shape[0]
    b0, b1 = (b_ref[k].reshape(cols, rank) for k in range(2))
    part = pl.ds(pl.multiple_of(section * cols, 128), cols)
    e = e_ref[:, part]
    c = c_ref[:, part]
    both = dot(c, jnp.concatenate([b0, b1], axis=1)).astype(BF16)
    pay_ref[pl.ds(0, rows), :] = dot(e, b0).astype(BF16)
    pay_ref[pl.ds(rows, rows), :] = both[:, :rank]
    pay_ref[pl.ds(2 * rows, rows), :] = both[:, rank:]
    square = dot(b0, b0, 0, 0)
    high = square.astype(BF16)
    pay_ref[pl.ds(3 * rows, rank), :] = high
    pay_ref[pl.ds(3 * rows + rank, rank), :] = (square - high.astype(F32)).astype(BF16)


def down_kernel(ids, e_ref, b_ref, early, late, early2, late2, pay_ref, a_ref):
    section, index = ids[0], ids[1]
    bit = lax.rem(lax.div(index, NEAR), 2)
    for k, mask in enumerate(DOWN_MASKS):
        holder = jnp.bitwise_xor(index, mask)
        blocks = (early, late, early2, late2)[k // 2]
        for j in range(2):
            panel = 2 * lax.div(holder, FAR) + jnp.bitwise_xor(bit, j)
            a_ref[panel, lax.rem(holder, 4)] = blocks[k % 2, j]
    cols = a_ref.shape[1] * a_ref.shape[2]
    rank = a_ref.shape[3]
    rows = e_ref.shape[0]
    p0, p1, q0, q1 = (a_ref[k].reshape(cols, rank) for k in range(4))
    w0 = (p0.astype(F32) + q0.astype(F32)).astype(BF16)
    w1 = (p1.astype(F32) + q1.astype(F32)).astype(BF16)
    e = e_ref[:, pl.ds(pl.multiple_of(section * cols, 128), cols)]
    both = dot(e, jnp.concatenate([w0, w1], axis=1)).astype(BF16)
    pay_ref[pl.ds(0, rows), :] = both[:, :rank]
    pay_ref[pl.ds(rows, rows), :] = both[:, rank:]
    b0 = b_ref[0].reshape(cols, rank)
    pay_ref[pl.ds(2 * rows, rank), :] = dot(b0, p1, 0, 0).astype(BF16)


def rows_kernel(
    ids, e_ref, c_ref, up_mine, up_other, down_mine, down_other, norm_ref, a_ref, b_ref,
    hkeep_ref, hsend_ref, akeep_ref, asend_ref, back_ref, v_ref, coef_ref, apan, hpan,
):
    section, index = ids[0], ids[1]
    rows, width = e_ref.shape
    cols = width // 2
    blk, rank = a_ref.shape[2:]

    def total(mine, other, start, size):
        part = pl.ds(start, size)
        return mine[part, :].astype(F32) + other[part, :].astype(F32)

    e0, y0, y1 = (total(up_mine, up_other, k * rows, rows) for k in range(3))
    square = total(up_mine, up_other, 3 * rows, rank)
    square = square + total(up_mine, up_other, 3 * rows + rank, rank)
    a0, a1 = (total(down_mine, down_other, k * rows, rows) for k in range(2))
    mixed = total(down_mine, down_other, 2 * rows, rank).astype(BF16)
    high = square.astype(BF16)
    low = (square - high.astype(F32)).astype(BF16)
    norm = norm_ref[...]
    scale = 1.0 / (2 * width)

    inv0 = lax.rsqrt(2.0 * norm * scale + epsilon)
    r0 = (inv0 * a0).astype(BF16)
    r0f = r0.astype(F32)
    r0s = dot(r0, high) + dot(r0, low)
    full = 2.0 * norm + jnp.sum(r0f * (2.0 * e0 + r0s), axis=1, keepdims=True)
    inv1 = lax.rsqrt(jnp.maximum(full, norm) * scale + epsilon)
    r1f = inv1 * (a1 + dot(r0, mixed))
    r1 = r1f.astype(BF16)
    m1 = jnp.sum(y1 * r1f, axis=1, keepdims=True) * scale
    c1 = inv1 * inv1 * m1
    v1 = (inv1 * y1).astype(BF16)
    u0 = y0 + dot(v1, mixed, 1, 1) - c1 * (e0 + r0s)
    m0 = jnp.sum(u0 * r0f, axis=1, keepdims=True) * scale
    c0 = inv0 * inv0 * m0
    v0 = (inv0 * u0).astype(BF16)

    part = pl.ds(pl.multiple_of(section * cols, 128), cols)
    e = e_ref[:, part]
    c = c_ref[:, part]
    b0 = b_ref[0].reshape(cols, rank)
    p1 = a_ref[1].reshape(cols, rank)
    h1f = e.astype(F32) + dot(r0, b0, 1, 1)
    backf = c.astype(F32) + dot(v1, p1, 1, 1) - c1 * h1f
    h1 = h1f.astype(BF16)
    back = backf.astype(BF16)
    back_ref[...] = back
    v_ref[0] = v0
    v_ref[1] = v1
    coef_ref[...] = jnp.broadcast_to(2.0 * c0 + c1, coef_ref.shape)

    hpan[0] = dot(back, r0, 0, 0).astype(BF16).reshape(8, blk // 2, rank)
    hpan[1] = dot(c, r1, 0, 0).astype(BF16).reshape(8, blk // 2, rank)
    both = dot(e, jnp.concatenate([v0, v1], axis=1), 0, 0).astype(BF16)
    g0 = both[:, :rank].reshape(4, blk, rank)
    apan[0] = g0
    apan[2] = g0
    apan[1] = dot(h1, v1, 0, 0).astype(BF16).reshape(4, blk, rank)
    apan[3] = both[:, rank:].reshape(4, blk, rank)

    bit = lax.rem(lax.div(index, NEAR), 2)
    for core, out in enumerate((hkeep_ref, hsend_ref)):
        for y in range(2):
            for near in range(2):
                place = lax.rem(jnp.bitwise_xor(index, core * CORE + y * Y + near * NEAR), 8)
                for j in range(2):
                    out[y, near, j] = hpan[jnp.bitwise_xor(section, j), place]
    for core, out in enumerate((akeep_ref, asend_ref)):
        for y in range(2):
            for far in range(2):
                holder = jnp.bitwise_xor(index, core * CORE + y * Y + far * FAR)
                for j in range(2):
                    panel = 2 * lax.div(holder, FAR) + jnp.bitwise_xor(bit, j)
                    out[y, far, j] = apan[panel, lax.rem(holder, 4)]


def embed_kernel(ids, e_ref, back_ref, v_ref, coef_ref, a_ref, out_ref):
    rows, cols = back_ref.shape
    rank = a_ref.shape[3]
    w0 = (a_ref[0].astype(F32) + a_ref[2].astype(F32)).astype(BF16).reshape(cols, rank)
    q1 = a_ref[3].reshape(cols, rank)
    e = e_ref[:, pl.ds(pl.multiple_of(ids[0] * cols, 128), cols)]
    out_ref[...] = (
        back_ref[...].astype(F32)
        + dot(v_ref[0], w0, 1, 1)
        + dot(v_ref[1], q1, 1, 1)
        - coef_ref[:, 0:1] * e.astype(F32)
    ).astype(BF16)


def grad_b_kernel(ids, early, late, out_ref, natural):
    section, index = ids[0], ids[1]
    for core, blocks in enumerate((early, late)):
        for k, mask in enumerate(UP_MASKS):
            place = lax.rem(jnp.bitwise_xor(index, mask | core), 8)
            for j in range(2):
                natural[8 * jnp.bitwise_xor(section, j) + place] = blocks[k, j]
    blocks, size, rank = natural.shape
    out_ref[...] = natural[...].reshape(blocks * size, rank).astype(F32).T


VMEM = pl.BlockSpec(memory_space=pltpu.VMEM)
SMEM = pl.BlockSpec(memory_space=pltpu.SMEM)
LIMIT = pltpu.CompilerParams(vmem_limit_bytes=40 * 1024 * 1024)


def call(kernel, ids, operands, outs, scratch=()):
    return pl.pallas_call(
        kernel,
        out_shape=[jax.ShapeDtypeStruct(shape, dtype) for shape, dtype in outs],
        in_specs=[SMEM] + [VMEM] * len(operands),
        out_specs=[VMEM] * len(outs),
        scratch_shapes=list(scratch),
        compiler_params=LIMIT,
    )(ids, *operands)


def paired(embeds, cotangent, adapter_a, adapter_b, norm_gains):
    section = lax.axis_index("section")
    index = lax.axis_index("dp")
    ids = jnp.stack([section, index]).astype(jnp.int32)
    rows, width = embeds.shape
    cols = width // 2
    down = adapter_a[0]
    blk, rank = down.shape
    half = blk // 2
    gain_row = lax.dynamic_index_in_dim(norm_gains, section, 0, keepdims=False)
    gain = lax.dynamic_slice_in_dim(gain_row, index * blk, blk, 0)[:, None]
    scaled = (down.astype(F32) * gain).astype(BF16)
    up = adapter_b[0].T
    norm = jnp.sum(jnp.square(embeds.astype(F32)), axis=1, keepdims=True)

    up_pair = jnp.stack([trade(up, FAR, turned), trade(up, FAR, spread)])
    down_pair = jnp.stack([trade(scaled, NEAR, turned), trade(scaled, NEAR, spread)])
    up_parts = gather_up(up_pair)
    down_parts = gather_down(down_pair)
    up_pay, b_all = call(
        up_kernel,
        ids,
        (embeds, cotangent, *up_parts),
        [((3 * rows + 2 * rank, rank), BF16), ((2, 8, half, rank), BF16)],
    )
    up_other = cross(up_pay)
    down_pay, a_all = call(
        down_kernel,
        ids,
        (embeds, b_all, *down_parts),
        [((2 * rows + rank, rank), BF16), ((4, 4, blk, rank), BF16)],
    )
    down_other = cross(down_pay)
    hkeep, hsend, akeep, asend, back, vees, coef = call(
        rows_kernel,
        ids,
        (embeds, cotangent, up_pay, up_other, down_pay, down_other, norm, a_all, b_all),
        [
            ((2, 2, 2, half, rank), BF16), ((2, 2, 2, half, rank), BF16),
            ((2, 2, 2, blk, rank), BF16), ((2, 2, 2, blk, rank), BF16),
            ((rows, cols), BF16), ((2, rows, rank), BF16), ((rows, rank), F32),
        ],
        [pltpu.VMEM((4, 4, blk, rank), BF16), pltpu.VMEM((2, 8, half, rank), BF16)],
    )

    h = add(hkeep, swap(hsend, CORE))
    h = add(h[0], swap(h[1], Y))
    h = add(h[0], swap(h[1], NEAR))
    h_own = add(h[0], swap(h[0], FAR))
    h_other = add(cross(h[1]), cross(h[1], FAR))
    grad_b_parts = gather_up(jnp.stack([h_own, h_other]))

    a = add(akeep, swap(asend, CORE))
    far = add(a[0, 1], swap(a[1, 1], Y))
    near = add(a[0, 0], swap(a[1, 0], Y))
    mine = add(near, swap(far, FAR))
    outer = trade(mine[0], NEAR, turned).astype(F32) + trade(mine[1], NEAR, joined).astype(F32)
    gain_part = jnp.sum(outer * down.astype(F32), axis=1)
    gain_other = cross(gain_part)
    first = jnp.where(section == 0, gain_part, gain_other)
    second = jnp.where(section == 0, gain_other, gain_part)

    (embed_cols,) = call(
        embed_kernel, ids, (embeds, back, vees, coef, a_all), [((rows, cols), BF16)]
    )
    (grad_b,) = call(
        grad_b_kernel,
        ids,
        grad_b_parts,
        [((rank, width), F32)],
        [pltpu.VMEM((16, half, rank), BF16)],
    )
    return ((gain * outer)[None], grad_b[None], jnp.stack([first, second]), embed_cols)


def general(embeds, cotangent, adapter_a, adapter_b, norm_gains):
    sections = lax.axis_size("section")
    section = lax.axis_index("section")
    index = lax.axis_index("dp")
    rows, width = embeds.shape
    cols = width // sections
    down = adapter_a[0]
    blk, rank = down.shape
    gain_row = lax.dynamic_index_in_dim(norm_gains, section % 2, 0, keepdims=False)
    gain = lax.dynamic_slice_in_dim(gain_row, index * blk, blk, 0)[:, None]
    scaled = (down.astype(F32) * gain).astype(BF16)
    down_all = lax.all_gather(lax.all_gather(scaled, "dp", axis=0, tiled=True), "section")
    up_all = lax.all_gather(lax.all_gather(adapter_b[0].T, "dp", axis=0, tiled=True), "section")
    start = section * cols
    tops = lax.dynamic_slice_in_dim(down_all, start, cols, 1)
    bottoms = lax.dynamic_slice_in_dim(down_all, width + start, cols, 1)
    ups = lax.dynamic_slice_in_dim(up_all, start, cols, 1)
    e = lax.dynamic_slice_in_dim(embeds, start, cols, 1)
    c = lax.dynamic_slice_in_dim(cotangent, start, cols, 1)
    norm = jnp.sum(jnp.square(embeds.astype(F32)), axis=1, keepdims=True)

    def project(left, right):
        return lax.dot_general(right, left, (((1,), (1,)), ((), ())), preferred_element_type=F32)

    def pairs(left, right):
        return jnp.einsum("tcr,ucq->turq", left, right, preferred_element_type=F32)

    lows, ups_e, ups_c, mixed, square = lax.psum(
        (
            project(e, tops) + project(e, bottoms),
            project(e, ups),
            project(c, ups),
            pairs(ups, tops),
            pairs(ups, ups),
        ),
        "section",
    )
    lows, ups_e, ups_c = (jnp.swapaxes(value, 1, 2) for value in (lows, ups_e, ups_c))
    scale = 1.0 / (2 * width)

    def exact(left, right):
        return jnp.dot(left, right, precision=lax.Precision.HIGHEST)

    reds, invs, spans = [], [], []
    for s in range(sections):
        full = 2.0 * norm
        low = lows[s]
        for t in range(s):
            red = reds[t].astype(F32)
            low = low + exact(red, mixed[t, s])
            full = full + jnp.sum(red * (2.0 * ups_e[t]), axis=1, keepdims=True)
            for q in range(s):
                other = exact(reds[q].astype(F32), square[q, t])
                full = full + jnp.sum(red * other, axis=1, keepdims=True)
        inv = lax.rsqrt(jnp.maximum(full, norm) * scale + epsilon)
        invs.append(inv)
        spans.append(inv * low)
        reds.append((inv * low).astype(BF16))
    vees, coefs = [None] * sections, [None] * sections
    for s in reversed(range(sections)):
        grad = ups_c[s]
        for t in range(s + 1, sections):
            hidden = ups_e[s]
            for q in range(t):
                hidden = hidden + exact(reds[q].astype(F32), square[q, s])
            grad = grad + exact(vees[t].astype(F32), mixed[s, t].T) - coefs[t] * hidden
        mean = jnp.sum(grad * spans[s], axis=1, keepdims=True) * scale
        coefs[s] = invs[s] * invs[s] * mean
        vees[s] = (invs[s] * grad).astype(BF16)
    hiddens = [e.astype(F32)]
    for s in range(sections - 1):
        hiddens.append(hiddens[s] + dot(reds[s], ups[s], 1, 1))
    back = c.astype(F32)
    embed_cols = jnp.zeros_like(back)
    terms = [None] * sections
    for s in reversed(range(sections)):
        h = hiddens[s].astype(BF16)
        terms[s] = jnp.stack(
            [
                dot(h, vees[s], 0, 0),
                dot(e, vees[s], 0, 0),
                dot(back.astype(BF16), reds[s], 0, 0),
            ]
        )
        embed_cols = embed_cols + dot(vees[s], bottoms[s], 1, 1) - coefs[s] * e.astype(F32)
        back = back + dot(vees[s], tops[s], 1, 1) - coefs[s] * hiddens[s]
    embed_cols = (embed_cols + back).astype(BF16)
    sums = lax.psum(jnp.stack(terms), "dp")
    mine = lax.all_to_all(sums, "section", 0, 2, tiled=True)[0]
    outer = lax.dynamic_slice_in_dim(mine[:2].reshape(2 * width, rank), index * blk, blk, 0)
    part = jnp.sum(outer * down.astype(F32), axis=1)
    parity = section % 2
    gain_pair = jnp.stack([jnp.where(parity == 0, part, 0.0), jnp.where(parity == 1, part, 0.0)])
    return ((gain * outer)[None], mine[2].T[None], lax.psum(gain_pair, "section"), embed_cols)


def solution(mesh):
    in_specs = (
        P("dp", None),
        P("dp", None),
        P("section", "dp", None),
        P("section", None, "dp"),
        P(),
    )
    out_specs = (
        P("section", "dp", None),
        P("section", None, None),
        P(None, "dp"),
        P("dp", "section"),
    )
    body = paired if mesh.shape["section"] == 2 and mesh.shape["dp"] == 16 else general
    return jax.shard_map(
        body, mesh=mesh, in_specs=in_specs, out_specs=out_specs, check_vma=False
    )
```

```python
import jax
import jax.numpy as jnp
from jax import lax
from jax.experimental import pallas as pl
from jax.experimental.pallas import tpu as pltpu
from jax.sharding import PartitionSpec as P

epsilon = 1e-05

F32 = jnp.float32
BF16 = jnp.bfloat16

CORE, Y, NEAR, FAR = 1, 2, 4, 8


def dot(left, right, left_dim=1, right_dim=0):
    return lax.dot_general(
        left, right, (((left_dim,), (right_dim,)), ((), ())), preferred_element_type=F32
    )


def swap(block, mask):
    count = lax.axis_size("dp")
    return lax.ppermute(block, "dp", [(i, i ^ mask) for i in range(count)])


def cross(block, mask):
    count = lax.axis_size("dp")
    route = [(i, (i + count) % (2 * count) ^ mask) for i in range(2 * count)]
    return lax.ppermute(block, ("section", "dp"), route)


def trade(block, mask, step):
    count = lax.axis_size("dp")
    route = []
    for section in range(2):
        for index in range(count):
            to_section, to_bit = step(section, int(bool(index & mask)))
            target = to_section * count + ((index & ~mask) | (mask if to_bit else 0))
            route.append((section * count + index, target))
    return lax.ppermute(block, ("section", "dp"), route)


def turned(s, b):
    return (b, s)


def spread(s, b):
    return (s, 1 - b) if s == b else (1 - s, b)


def joined(s, b):
    return (1 - s, b) if s == b else (s, 1 - b)


def add(left, right):
    return (left.astype(F32) + right.astype(F32)).astype(BF16)


def gather_up(pair):
    side = swap(pair, Y)
    near = swap(pair, NEAR)
    both = swap(pair, NEAR | Y)
    chips = (pair, near, side, both)
    return *chips, *(swap(block, CORE) for block in chips)


UP_MASKS = (0, NEAR, Y, NEAR | Y, CORE, CORE | NEAR, CORE | Y, CORE | NEAR | Y)


def gather_down(pair):
    far = swap(pair, FAR)
    chips = (pair, swap(pair, Y), far, swap(far, Y))
    return *chips, *(swap(block, CORE) for block in chips)


DOWN_MASKS = (0, Y, FAR, FAR | Y, CORE, CORE | Y, CORE | FAR, CORE | FAR | Y)


def up_kernel(e_ref, c_ref, *refs):
    *blocks, pay_ref, b_ref, norm_ref = refs
    section, index = lax.axis_index("section"), lax.axis_index("dp")
    bit = lax.rem(lax.div(index, FAR), 2)
    for block, mask in zip(blocks, UP_MASKS):
        place = lax.rem(jnp.bitwise_xor(index, mask), 8)
        for j in range(2):
            b_ref[jnp.bitwise_xor(bit, j), place] = block[j]
    norm_ref[...] = jnp.sum(jnp.square(e_ref[...].astype(F32)), axis=1, keepdims=True)
    cols = b_ref.shape[1] * b_ref.shape[2]
    rank = b_ref.shape[3]
    rows = e_ref.shape[0]
    b0, b1 = (b_ref[k].reshape(cols, rank) for k in range(2))
    part = pl.ds(pl.multiple_of(section * cols, 128), cols)
    e = e_ref[:, part]
    c = c_ref[:, part]
    both = dot(c, jnp.concatenate([b0, b1], axis=1)).astype(BF16)
    pay_ref[pl.ds(0, rows), :] = dot(e, b0).astype(BF16)
    pay_ref[pl.ds(rows, rows), :] = both[:, :rank]
    pay_ref[pl.ds(2 * rows, rows), :] = both[:, rank:]
    square = dot(b0, b0, 0, 0)
    high = square.astype(BF16)
    pay_ref[pl.ds(3 * rows, rank), :] = high
    pay_ref[pl.ds(3 * rows + rank, rank), :] = (square - high.astype(F32)).astype(BF16)


def down_kernel(e_ref, b_ref, *refs):
    *blocks, pay_ref, a_ref = refs
    section, index = lax.axis_index("section"), lax.axis_index("dp")
    bit = lax.rem(lax.div(index, NEAR), 2)
    for block, mask in zip(blocks, DOWN_MASKS):
        holder = jnp.bitwise_xor(index, mask)
        for j in range(2):
            panel = 2 * lax.div(holder, FAR) + jnp.bitwise_xor(bit, j)
            a_ref[panel, lax.rem(holder, 4)] = block[j]
    cols = a_ref.shape[1] * a_ref.shape[2]
    rank = a_ref.shape[3]
    rows = e_ref.shape[0]
    p0, p1, q0, q1 = (a_ref[k].reshape(cols, rank) for k in range(4))
    w0 = (p0.astype(F32) + q0.astype(F32)).astype(BF16)
    w1 = (p1.astype(F32) + q1.astype(F32)).astype(BF16)
    e = e_ref[:, pl.ds(pl.multiple_of(section * cols, 128), cols)]
    both = dot(e, jnp.concatenate([w0, w1], axis=1)).astype(BF16)
    pay_ref[pl.ds(0, rows), :] = both[:, :rank]
    pay_ref[pl.ds(rows, rows), :] = both[:, rank:]
    b0 = b_ref[0].reshape(cols, rank)
    pay_ref[pl.ds(2 * rows, rank), :] = dot(b0, p1, 0, 0).astype(BF16)


def rows_kernel(
    e_ref, c_ref, up_mine, up_other, down_mine, down_other, norm_ref, a_ref, b_ref,
    hkeep_ref, hsend_ref, akeep_ref, asend_ref, back_ref, v_ref, coef_ref, apan, hpan,
):
    section, index = lax.axis_index("section"), lax.axis_index("dp")
    rows, width = e_ref.shape
    cols = width // 2
    blk, rank = a_ref.shape[2:]

    def total(mine, other, start, size):
        part = pl.ds(start, size)
        return mine[part, :].astype(F32) + other[part, :].astype(F32)

    e0, y0, y1 = (total(up_mine, up_other, k * rows, rows) for k in range(3))
    square = total(up_mine, up_other, 3 * rows, rank)
    square = square + total(up_mine, up_other, 3 * rows + rank, rank)
    a0, a1 = (total(down_mine, down_other, k * rows, rows) for k in range(2))
    mixed = total(down_mine, down_other, 2 * rows, rank).astype(BF16)
    high = square.astype(BF16)
    low = (square - high.astype(F32)).astype(BF16)
    norm = norm_ref[...]
    scale = 1.0 / (2 * width)

    inv0 = lax.rsqrt(2.0 * norm * scale + epsilon)
    r0 = (inv0 * a0).astype(BF16)
    r0f = r0.astype(F32)
    r0s = dot(r0, high) + dot(r0, low)
    full = 2.0 * norm + jnp.sum(r0f * (2.0 * e0 + r0s), axis=1, keepdims=True)
    inv1 = lax.rsqrt(jnp.maximum(full, norm) * scale + epsilon)
    r1f = inv1 * (a1 + dot(r0, mixed))
    r1 = r1f.astype(BF16)
    m1 = jnp.sum(y1 * r1f, axis=1, keepdims=True) * scale
    c1 = inv1 * inv1 * m1
    v1 = (inv1 * y1).astype(BF16)
    u0 = y0 + dot(v1, mixed, 1, 1) - c1 * (e0 + r0s)
    m0 = jnp.sum(u0 * r0f, axis=1, keepdims=True) * scale
    c0 = inv0 * inv0 * m0
    v0 = (inv0 * u0).astype(BF16)

    part = pl.ds(pl.multiple_of(section * cols, 128), cols)
    e = e_ref[:, part]
    c = c_ref[:, part]
    b0 = b_ref[0].reshape(cols, rank)
    p1 = a_ref[1].reshape(cols, rank)
    h1f = e.astype(F32) + dot(r0, b0, 1, 1)
    backf = c.astype(F32) + dot(v1, p1, 1, 1) - c1 * h1f
    h1 = h1f.astype(BF16)
    back = backf.astype(BF16)
    back_ref[...] = back
    v_ref[0] = v0
    v_ref[1] = v1
    coef_ref[...] = jnp.broadcast_to(2.0 * c0 + c1, coef_ref.shape)

    hpan[0] = dot(back, r0, 0, 0).astype(BF16).reshape(8, blk // 2, rank)
    hpan[1] = dot(c, r1, 0, 0).astype(BF16).reshape(8, blk // 2, rank)
    both = dot(e, jnp.concatenate([v0, v1], axis=1), 0, 0).astype(BF16)
    g0 = both[:, :rank].reshape(4, blk, rank)
    apan[0] = g0
    apan[2] = g0
    apan[1] = dot(h1, v1, 0, 0).astype(BF16).reshape(4, blk, rank)
    apan[3] = both[:, rank:].reshape(4, blk, rank)

    bit = lax.rem(lax.div(index, NEAR), 2)
    for core, out in enumerate((hkeep_ref, hsend_ref)):
        for y in range(2):
            for near in range(2):
                place = lax.rem(jnp.bitwise_xor(index, core * CORE + y * Y + near * NEAR), 8)
                for j in range(2):
                    out[y, near, j] = hpan[jnp.bitwise_xor(section, j), place]
    for core, out in enumerate((akeep_ref, asend_ref)):
        for y in range(2):
            for far in range(2):
                holder = jnp.bitwise_xor(index, core * CORE + y * Y + far * FAR)
                for j in range(2):
                    panel = 2 * lax.div(holder, FAR) + jnp.bitwise_xor(bit, j)
                    out[y, far, j] = apan[panel, lax.rem(holder, 4)]


def embed_kernel(e_ref, back_ref, v_ref, coef_ref, a_ref, out_ref):
    _, cols = back_ref.shape
    rank = a_ref.shape[3]
    w0 = (a_ref[0].astype(F32) + a_ref[2].astype(F32)).astype(BF16).reshape(cols, rank)
    q1 = a_ref[3].reshape(cols, rank)
    section = lax.axis_index("section")
    e = e_ref[:, pl.ds(pl.multiple_of(section * cols, 128), cols)]
    out_ref[...] = (
        back_ref[...].astype(F32)
        + dot(v_ref[0], w0, 1, 1)
        + dot(v_ref[1], q1, 1, 1)
        - coef_ref[:, 0:1] * e.astype(F32)
    ).astype(BF16)


def grad_b_kernel(*refs):
    *parts, out_ref, natural = refs
    section, index = lax.axis_index("section"), lax.axis_index("dp")
    for part, mask in zip(parts, UP_MASKS):
        place = lax.rem(jnp.bitwise_xor(index, mask), 8)
        for j in range(2):
            natural[8 * jnp.bitwise_xor(section, j) + place] = part[j]
    blocks, size, rank = natural.shape
    out_ref[...] = natural[...].reshape(blocks * size, rank).astype(F32).T


def last_kernel(near_ref, far_ref, a_ref, out0_ref, out1_ref):
    index = lax.axis_index("dp")
    bit = lax.rem(lax.div(index, NEAR), 2)
    blk, rank = a_ref.shape[2:]
    spare = -blk % rank
    row = lax.broadcasted_iota(jnp.int32, (out0_ref.shape[0] - blk, rank), 0)
    tail = jnp.zeros(row.shape, F32)
    ones = jnp.ones((8, rank), F32)
    chunks = (blk + spare) // rank
    for k, out in enumerate((out0_ref, out1_ref)):
        call_id = jnp.bitwise_xor(bit, k)
        mine = near_ref[k].astype(F32) + far_ref[k].astype(F32)
        out[pl.ds(0, blk), :] = mine.astype(BF16)
        terms = mine * a_ref[2 * lax.div(index, FAR) + call_id, lax.rem(index, 4)].astype(F32)
        terms = jnp.concatenate([terms, jnp.zeros((spare, rank), F32)])
        sums = lax.dot_general(
            ones, terms, (((1,), (1,)), ((), ())),
            precision=lax.Precision.HIGHEST, preferred_element_type=F32,
        )
        for i in range(chunks):
            piece = jnp.broadcast_to(sums[0:1, i * rank : (i + 1) * rank], row.shape)
            tail = jnp.where(row == call_id * chunks + i, piece, tail)
    for out in (out0_ref, out1_ref):
        out[pl.ds(blk, tail.shape[0]), :] = tail.astype(BF16)


def grad_a_kernel(first_ref, second_ref, column_ref, gains_ref, out_ref, gain_ref):
    blk, rank = out_ref.shape
    total = first_ref[...].astype(F32) + second_ref[...].astype(F32)
    out_ref[...] = column_ref[...] * total[:blk]
    chunks = pl.cdiv(blk, rank)
    for k in range(2):
        for i in range(chunks):
            size = min(rank, blk - i * rank)
            part = pl.ds(i * rank, size)
            line = total[blk + k * chunks + i : blk + k * chunks + i + 1, :size]
            gain_ref[pl.ds(k, 1), part] = line / gains_ref[pl.ds(k, 1), part]


VMEM = pl.BlockSpec(memory_space=pltpu.VMEM)


def call(kernel, operands, outs, scratch=(), limit=16):
    return pl.pallas_call(
        kernel,
        out_shape=[jax.ShapeDtypeStruct(shape, dtype) for shape, dtype in outs],
        in_specs=[VMEM] * len(operands),
        out_specs=[VMEM] * len(outs),
        scratch_shapes=list(scratch),
        compiler_params=pltpu.CompilerParams(vmem_limit_bytes=limit * 1024 * 1024),
    )(*operands)


def paired(embeds, cotangent, adapter_a, adapter_b, norm_gains):
    return paired_body(embeds, cotangent, adapter_a, adapter_b, norm_gains)


def paired_body(embeds, cotangent, adapter_a, adapter_b, norm_gains):
    section = lax.axis_index("section")
    index = lax.axis_index("dp")
    rows, width = embeds.shape
    cols = width // 2
    down = adapter_a[0]
    blk, rank = down.shape
    half = blk // 2
    gains = lax.dynamic_slice_in_dim(norm_gains, index * blk, blk, 1)
    gain = jnp.where(section == 0, gains[0], gains[1])[:, None]
    scaled = (down.astype(F32) * gain).astype(BF16)
    up = adapter_b[0].T

    a_spread = trade(scaled, NEAR, spread)
    a_turn = trade(scaled, NEAR, turned)
    b_spread = trade(up, FAR, spread)
    b_turn = trade(up, FAR, turned)
    down_pair = jnp.stack([a_turn, a_spread])
    up_pair = jnp.stack([b_turn, b_spread])
    up_parts = gather_up(up_pair)
    down_parts = gather_down(down_pair)
    up_pay, b_all, norm = call(
        up_kernel,
        (embeds, cotangent, *up_parts),
        [
            ((3 * rows + 2 * rank, rank), BF16),
            ((2, 8, half, rank), BF16),
            ((rows, 1), F32),
        ],
    )
    up_other = cross(up_pay, 0)
    down_pay, a_all = call(
        down_kernel,
        (embeds, b_all, *down_parts),
        [((2 * rows + rank, rank), BF16), ((4, 4, blk, rank), BF16)],
    )
    down_other = cross(down_pay, 0)
    hkeep, hsend, akeep, asend, back, vees, coef = call(
        rows_kernel,
        (embeds, cotangent, up_pay, up_other, down_pay, down_other, norm, a_all, b_all),
        [
            ((2, 2, 2, half, rank), BF16), ((2, 2, 2, half, rank), BF16),
            ((2, 2, 2, blk, rank), BF16), ((2, 2, 2, blk, rank), BF16),
            ((rows, cols), BF16), ((2, rows, rank), BF16), ((rows, rank), F32),
        ],
        [pltpu.VMEM((4, 4, blk, rank), BF16), pltpu.VMEM((2, 8, half, rank), BF16)],
        24,
    )

    recv = swap(hsend, CORE)
    h_side = add(hkeep[1], recv[1])
    h_mine = add(hkeep[0], recv[0])
    recv = swap(asend, CORE)
    g_far_side = add(akeep[1, 1], recv[1, 1])
    g_side = add(akeep[1, 0], recv[1, 0])
    g_mine = add(akeep[0], recv[0])
    recv = swap(h_side, Y)
    h_near = add(h_mine[1], recv[1])
    h_mine = add(h_mine[0], recv[0])
    recv = swap(h_near, NEAR)
    h_own = add(h_mine[0], recv[0])
    h_other = add(h_mine[1], recv[1])
    h_own = add(h_own, swap(h_own, FAR))
    h_other = add(cross(h_other, FAR), cross(h_other, 0))
    grad_b_parts = gather_up(jnp.stack([h_own, h_other]))

    far = add(g_mine[1], swap(g_far_side, Y))
    near = add(g_mine[0], swap(g_side, Y))
    tall = ((blk + 16, rank), BF16)
    turn_out, join_out = call(last_kernel, (near, swap(far, FAR), a_all), [tall, tall])
    grad_a, grad_gain = call(
        grad_a_kernel,
        (trade(turn_out, NEAR, turned), trade(join_out, NEAR, joined), gain, gains),
        [((blk, rank), F32), ((2, blk), F32)],
    )
    (embed_cols,) = call(embed_kernel, (embeds, back, vees, coef, a_all), [((rows, cols), BF16)])
    (grad_b,) = call(
        grad_b_kernel, grad_b_parts, [((rank, width), F32)], [pltpu.VMEM((16, half, rank), BF16)]
    )
    return (grad_a[None], grad_b[None], grad_gain, embed_cols)


def general(embeds, cotangent, adapter_a, adapter_b, norm_gains):
    sections = lax.axis_size("section")
    section = lax.axis_index("section")
    index = lax.axis_index("dp")
    _, width = embeds.shape
    cols = width // sections
    down = adapter_a[0]
    blk, rank = down.shape
    gain_row = lax.dynamic_index_in_dim(norm_gains, section % 2, 0, keepdims=False)
    gain = lax.dynamic_slice_in_dim(gain_row, index * blk, blk, 0)[:, None]
    scaled = (down.astype(F32) * gain).astype(BF16)
    down_all = lax.all_gather(lax.all_gather(scaled, "dp", axis=0, tiled=True), "section")
    up_all = lax.all_gather(lax.all_gather(adapter_b[0].T, "dp", axis=0, tiled=True), "section")
    start = section * cols
    tops = lax.dynamic_slice_in_dim(down_all, start, cols, 1)
    bottoms = lax.dynamic_slice_in_dim(down_all, width + start, cols, 1)
    ups = lax.dynamic_slice_in_dim(up_all, start, cols, 1)
    e = lax.dynamic_slice_in_dim(embeds, start, cols, 1)
    c = lax.dynamic_slice_in_dim(cotangent, start, cols, 1)
    norm = jnp.sum(jnp.square(embeds.astype(F32)), axis=1, keepdims=True)

    def project(left, right):
        return lax.dot_general(right, left, (((1,), (1,)), ((), ())), preferred_element_type=F32)

    def pairs(left, right):
        return jnp.einsum("tcr,ucq->turq", left, right, preferred_element_type=F32)

    lows, ups_e, ups_c, mixed, square = lax.psum(
        (
            project(e, tops) + project(e, bottoms),
            project(e, ups),
            project(c, ups),
            pairs(ups, tops),
            pairs(ups, ups),
        ),
        "section",
    )
    lows, ups_e, ups_c = (jnp.swapaxes(value, 1, 2) for value in (lows, ups_e, ups_c))
    scale = 1.0 / (2 * width)

    def exact(left, right):
        return jnp.dot(left, right, precision=lax.Precision.HIGHEST)

    reds, invs, spans = [], [], []
    for s in range(sections):
        full = 2.0 * norm
        low = lows[s]
        for t in range(s):
            red = reds[t].astype(F32)
            low = low + exact(red, mixed[t, s])
            full = full + jnp.sum(red * (2.0 * ups_e[t]), axis=1, keepdims=True)
            for q in range(s):
                other = exact(reds[q].astype(F32), square[q, t])
                full = full + jnp.sum(red * other, axis=1, keepdims=True)
        inv = lax.rsqrt(jnp.maximum(full, norm) * scale + epsilon)
        invs.append(inv)
        spans.append(inv * low)
        reds.append((inv * low).astype(BF16))
    vees, coefs = [None] * sections, [None] * sections
    for s in reversed(range(sections)):
        grad = ups_c[s]
        for t in range(s + 1, sections):
            hidden = ups_e[s]
            for q in range(t):
                hidden = hidden + exact(reds[q].astype(F32), square[q, s])
            grad = grad + exact(vees[t].astype(F32), mixed[s, t].T) - coefs[t] * hidden
        mean = jnp.sum(grad * spans[s], axis=1, keepdims=True) * scale
        coefs[s] = invs[s] * invs[s] * mean
        vees[s] = (invs[s] * grad).astype(BF16)
    hiddens = [e.astype(F32)]
    for s in range(sections - 1):
        hiddens.append(hiddens[s] + dot(reds[s], ups[s], 1, 1))
    back = c.astype(F32)
    embed_cols = jnp.zeros_like(back)
    terms = [None] * sections
    for s in reversed(range(sections)):
        h = hiddens[s].astype(BF16)
        terms[s] = jnp.stack(
            [
                dot(h, vees[s], 0, 0),
                dot(e, vees[s], 0, 0),
                dot(back.astype(BF16), reds[s], 0, 0),
            ]
        )
        embed_cols = embed_cols + dot(vees[s], bottoms[s], 1, 1) - coefs[s] * e.astype(F32)
        back = back + dot(vees[s], tops[s], 1, 1) - coefs[s] * hiddens[s]
    embed_cols = (embed_cols + back).astype(BF16)
    sums = lax.psum(jnp.stack(terms), "dp")
    mine = lax.all_to_all(sums, "section", 0, 2, tiled=True)[0]
    outer = lax.dynamic_slice_in_dim(mine[:2].reshape(2 * width, rank), index * blk, blk, 0)
    part = jnp.sum(outer * down.astype(F32), axis=1)
    parity = section % 2
    gain_pair = jnp.stack([jnp.where(parity == 0, part, 0.0), jnp.where(parity == 1, part, 0.0)])
    return ((gain * outer)[None], mine[2].T[None], lax.psum(gain_pair, "section"), embed_cols)


def solution(mesh):
    in_specs = (
        P("dp", None),
        P("dp", None),
        P("section", "dp", None),
        P("section", None, "dp"),
        P(),
    )
    out_specs = (
        P("section", "dp", None),
        P("section", None, None),
        P(None, "dp"),
        P("dp", "section"),
    )
    fast = mesh.shape["section"] == 2 and mesh.shape["dp"] == 16
    return jax.shard_map(
        paired if fast else general,
        mesh=mesh,
        in_specs=in_specs,
        out_specs=out_specs,
        check_vma=False,
    )
```

```python
import jax
import jax.numpy as jnp
from jax import lax
from jax.experimental import pallas as pl
from jax.experimental.pallas import tpu as pltpu
from jax.sharding import PartitionSpec as P

epsilon = 1e-05

F32 = jnp.float32
BF16 = jnp.bfloat16

CORE, Y, NEAR, FAR = 1, 2, 4, 8


def dot(left, right, left_dim=1, right_dim=0):
    return lax.dot_general(
        left, right, (((left_dim,), (right_dim,)), ((), ())), preferred_element_type=F32
    )


def swap(block, mask):
    count = lax.axis_size("dp")
    return lax.ppermute(block, "dp", [(i, i ^ mask) for i in range(count)])


def cross(block, mask):
    count = lax.axis_size("dp")
    route = [(i, (i + count) % (2 * count) ^ mask) for i in range(2 * count)]
    return lax.ppermute(block, ("section", "dp"), route)


def trade(block, mask, step):
    count = lax.axis_size("dp")
    route = []
    for section in range(2):
        for index in range(count):
            to_section, to_bit = step(section, int(bool(index & mask)))
            target = to_section * count + ((index & ~mask) | (mask if to_bit else 0))
            route.append((section * count + index, target))
    return lax.ppermute(block, ("section", "dp"), route)


def turned(s, b):
    return (b, s)


def spread(s, b):
    return (s, 1 - b) if s == b else (1 - s, b)


def joined(s, b):
    return (1 - s, b) if s == b else (s, 1 - b)


def add(left, right):
    return (left.astype(F32) + right.astype(F32)).astype(BF16)


def gather_up(pair):
    side = swap(pair, Y)
    near = swap(pair, NEAR)
    both = swap(pair, NEAR | Y)
    chips = (pair, near, side, both)
    return *chips, *(swap(block, CORE) for block in chips)


UP_MASKS = (0, NEAR, Y, NEAR | Y, CORE, CORE | NEAR, CORE | Y, CORE | NEAR | Y)


def gather_down(pair):
    far = swap(pair, FAR)
    chips = (pair, swap(pair, Y), far, swap(far, Y))
    return *chips, *(swap(block, CORE) for block in chips)


DOWN_MASKS = (0, Y, FAR, FAR | Y, CORE, CORE | Y, CORE | FAR, CORE | FAR | Y)


def half_kernel(e_all, c_all, e_ref, c_ref, norm_ref):
    half = e_ref.shape[1]
    columns = pl.ds(pl.multiple_of(lax.axis_index("section") * half, 128), half)
    e_ref[...] = e_all[:, columns]
    c_ref[...] = c_all[:, columns]
    norm_ref[...] = jnp.sum(jnp.square(e_all[...].astype(F32)), axis=1, keepdims=True)


def up_kernel(e_ref, c_ref, *refs):
    *blocks, pay_ref, b_ref = refs
    index = lax.axis_index("dp")
    bit = lax.rem(lax.div(index, FAR), 2)
    for block, mask in zip(blocks, UP_MASKS):
        place = lax.rem(jnp.bitwise_xor(index, mask), 8)
        for j in range(2):
            b_ref[jnp.bitwise_xor(bit, j), place] = block[j]
    cols = b_ref.shape[1] * b_ref.shape[2]
    rank = b_ref.shape[3]
    rows = e_ref.shape[0]
    b0, b1 = (b_ref[k].reshape(cols, rank) for k in range(2))
    square = dot(b0, b0, 0, 0)
    e = e_ref[...]
    c = c_ref[...]
    both = dot(c, jnp.concatenate([b0, b1], axis=1)).astype(BF16)
    pay_ref[pl.ds(0, rows), :] = dot(e, b0).astype(BF16)
    pay_ref[pl.ds(rows, rows), :] = both[:, :rank]
    pay_ref[pl.ds(2 * rows, rows), :] = both[:, rank:]
    high = square.astype(BF16)
    pay_ref[pl.ds(3 * rows, rank), :] = high
    pay_ref[pl.ds(3 * rows + rank, rank), :] = (square - high.astype(F32)).astype(BF16)


def down_kernel(e_ref, b_ref, *refs):
    *blocks, pay_ref, a_ref = refs
    index = lax.axis_index("dp")
    bit = lax.rem(lax.div(index, NEAR), 2)
    for block, mask in zip(blocks, DOWN_MASKS):
        holder = jnp.bitwise_xor(index, mask)
        for j in range(2):
            panel = 2 * lax.div(holder, FAR) + jnp.bitwise_xor(bit, j)
            a_ref[panel, lax.rem(holder, 4)] = block[j]
    cols = a_ref.shape[1] * a_ref.shape[2]
    rank = a_ref.shape[3]
    rows = e_ref.shape[0]
    p0, p1, q0, q1 = (a_ref[k].reshape(cols, rank) for k in range(4))
    w0 = (p0.astype(F32) + q0.astype(F32)).astype(BF16)
    w1 = (p1.astype(F32) + q1.astype(F32)).astype(BF16)
    e = e_ref[...]
    both = dot(e, jnp.concatenate([w0, w1], axis=1)).astype(BF16)
    pay_ref[pl.ds(0, rows), :] = both[:, :rank]
    pay_ref[pl.ds(rows, rows), :] = both[:, rank:]
    b0 = b_ref[0].reshape(cols, rank)
    pay_ref[pl.ds(2 * rows, rank), :] = dot(b0, p1, 0, 0).astype(BF16)


def rows_kernel(
    e_ref, c_ref, up_mine, up_other, down_mine, down_other, norm_ref, a_ref, b_ref,
    hkeep_ref, hsend_ref, akeep_ref, asend_ref, back_ref, v_ref, coef_ref, apan, hpan,
):
    section, index = lax.axis_index("section"), lax.axis_index("dp")
    rows, cols = e_ref.shape
    width = 2 * cols
    blk, rank = a_ref.shape[2:]

    def total(mine, other, start, size):
        part = pl.ds(start, size)
        return mine[part, :].astype(F32) + other[part, :].astype(F32)

    e0, y0, y1 = (total(up_mine, up_other, k * rows, rows) for k in range(3))
    square = total(up_mine, up_other, 3 * rows, rank)
    square = square + total(up_mine, up_other, 3 * rows + rank, rank)
    a0, a1 = (total(down_mine, down_other, k * rows, rows) for k in range(2))
    mixed = total(down_mine, down_other, 2 * rows, rank).astype(BF16)
    high = square.astype(BF16)
    low = (square - high.astype(F32)).astype(BF16)
    norm = norm_ref[...]
    scale = 1.0 / (2 * width)

    inv0 = lax.rsqrt(2.0 * norm * scale + epsilon)
    r0 = (inv0 * a0).astype(BF16)
    r0f = r0.astype(F32)
    r0s = dot(r0, high) + dot(r0, low)
    full = 2.0 * norm + jnp.sum(r0f * (2.0 * e0 + r0s), axis=1, keepdims=True)
    inv1 = lax.rsqrt(jnp.maximum(full, norm) * scale + epsilon)
    r1f = inv1 * (a1 + dot(r0, mixed))
    r1 = r1f.astype(BF16)
    m1 = jnp.sum(y1 * r1f, axis=1, keepdims=True) * scale
    c1 = inv1 * inv1 * m1
    v1 = (inv1 * y1).astype(BF16)
    u0 = y0 + dot(v1, mixed, 1, 1) - c1 * (e0 + r0s)
    m0 = jnp.sum(u0 * r0f, axis=1, keepdims=True) * scale
    c0 = inv0 * inv0 * m0
    v0 = (inv0 * u0).astype(BF16)

    e = e_ref[...]
    c = c_ref[...]
    b0 = b_ref[0].reshape(cols, rank)
    p1 = a_ref[1].reshape(cols, rank)
    h1f = e.astype(F32) + dot(r0, b0, 1, 1)
    backf = c.astype(F32) + dot(v1, p1, 1, 1) - c1 * h1f
    h1 = h1f.astype(BF16)
    back = backf.astype(BF16)
    back_ref[...] = back
    v_ref[0] = v0
    v_ref[1] = v1
    coef_ref[...] = jnp.broadcast_to(2.0 * c0 + c1, coef_ref.shape)

    hpan[0] = dot(back, r0, 0, 0).astype(BF16).reshape(8, blk // 2, rank)
    hpan[1] = dot(c, r1, 0, 0).astype(BF16).reshape(8, blk // 2, rank)
    both = dot(e, jnp.concatenate([v0, v1], axis=1), 0, 0).astype(BF16)
    g0 = both[:, :rank].reshape(4, blk, rank)
    apan[0] = g0
    apan[2] = g0
    apan[1] = dot(h1, v1, 0, 0).astype(BF16).reshape(4, blk, rank)
    apan[3] = both[:, rank:].reshape(4, blk, rank)

    bit = lax.rem(lax.div(index, NEAR), 2)
    for core, out in enumerate((hkeep_ref, hsend_ref)):
        for y in range(2):
            for near in range(2):
                place = lax.rem(jnp.bitwise_xor(index, core * CORE + y * Y + near * NEAR), 8)
                for j in range(2):
                    out[y, near, j] = hpan[jnp.bitwise_xor(section, j), place]
    for core, out in enumerate((akeep_ref, asend_ref)):
        for y in range(2):
            for far in range(2):
                holder = jnp.bitwise_xor(index, core * CORE + y * Y + far * FAR)
                for j in range(2):
                    panel = 2 * lax.div(holder, FAR) + jnp.bitwise_xor(bit, j)
                    out[y, far, j] = apan[panel, lax.rem(holder, 4)]


def embed_kernel(e_ref, back_ref, v_ref, coef_ref, a_ref, out_ref):
    _, cols = back_ref.shape
    rank = a_ref.shape[3]
    w0 = (a_ref[0].astype(F32) + a_ref[2].astype(F32)).astype(BF16).reshape(cols, rank)
    q1 = a_ref[3].reshape(cols, rank)
    e = e_ref[...]
    out_ref[...] = (
        back_ref[...].astype(F32)
        + dot(v_ref[0], w0, 1, 1)
        + dot(v_ref[1], q1, 1, 1)
        - coef_ref[:, 0:1] * e.astype(F32)
    ).astype(BF16)


def grad_b_kernel(*refs):
    *parts, out_ref, natural = refs
    section, index = lax.axis_index("section"), lax.axis_index("dp")
    for part, mask in zip(parts, UP_MASKS):
        place = lax.rem(jnp.bitwise_xor(index, mask), 8)
        for j in range(2):
            natural[8 * jnp.bitwise_xor(section, j) + place] = part[j]
    blocks, size, rank = natural.shape
    out_ref[...] = natural[...].reshape(blocks * size, rank).astype(F32).T


def last_kernel(near_ref, side_ref, far_ref, a_ref, out0_ref, out1_ref):
    index = lax.axis_index("dp")
    bit = lax.rem(lax.div(index, NEAR), 2)
    blk, rank = a_ref.shape[2:]
    spare = -blk % rank
    row = lax.broadcasted_iota(jnp.int32, (out0_ref.shape[0] - blk, rank), 0)
    tail = jnp.zeros(row.shape, F32)
    ones = jnp.ones((8, rank), F32)
    chunks = (blk + spare) // rank
    for k, out in enumerate((out0_ref, out1_ref)):
        call_id = jnp.bitwise_xor(bit, k)
        mine = near_ref[k].astype(F32) + side_ref[k].astype(F32) + far_ref[k].astype(F32)
        out[pl.ds(0, blk), :] = mine.astype(BF16)
        terms = mine * a_ref[2 * lax.div(index, FAR) + call_id, lax.rem(index, 4)].astype(F32)
        terms = jnp.concatenate([terms, jnp.zeros((spare, rank), F32)])
        sums = lax.dot_general(
            ones, terms, (((1,), (1,)), ((), ())),
            precision=lax.Precision.HIGHEST, preferred_element_type=F32,
        )
        for i in range(chunks):
            piece = jnp.broadcast_to(sums[0:1, i * rank : (i + 1) * rank], row.shape)
            tail = jnp.where(row == call_id * chunks + i, piece, tail)
    for out in (out0_ref, out1_ref):
        out[pl.ds(blk, tail.shape[0]), :] = tail.astype(BF16)


def grad_a_kernel(first_ref, second_ref, column_ref, gains_ref, out_ref, gain_ref):
    blk, rank = out_ref.shape
    total = first_ref[...].astype(F32) + second_ref[...].astype(F32)
    out_ref[...] = column_ref[...] * total[:blk]
    chunks = pl.cdiv(blk, rank)
    for k in range(2):
        for i in range(chunks):
            size = min(rank, blk - i * rank)
            part = pl.ds(i * rank, size)
            line = total[blk + k * chunks + i : blk + k * chunks + i + 1, :size]
            gain_ref[pl.ds(k, 1), part] = line / gains_ref[pl.ds(k, 1), part]


VMEM = pl.BlockSpec(memory_space=pltpu.VMEM)


def call(kernel, operands, outs, scratch=(), limit=16):
    return pl.pallas_call(
        kernel,
        out_shape=[jax.ShapeDtypeStruct(shape, dtype) for shape, dtype in outs],
        in_specs=[VMEM] * len(operands),
        out_specs=[VMEM] * len(outs),
        scratch_shapes=list(scratch),
        compiler_params=pltpu.CompilerParams(vmem_limit_bytes=limit * 1024 * 1024),
    )(*operands)


def paired(embeds, cotangent, adapter_a, adapter_b, norm_gains):
    return paired_body(embeds, cotangent, adapter_a, adapter_b, norm_gains)


def paired_body(embeds, cotangent, adapter_a, adapter_b, norm_gains):
    section = lax.axis_index("section")
    index = lax.axis_index("dp")
    rows, width = embeds.shape
    cols = width // 2
    down = adapter_a[0]
    blk, rank = down.shape
    half = blk // 2
    gains = lax.dynamic_slice_in_dim(norm_gains, index * blk, blk, 1)
    gain = jnp.where(section == 0, gains[0], gains[1])[:, None]
    place = index - lax.rem(lax.div(index, NEAR), 2) * NEAR + section * NEAR
    pair_gains = lax.dynamic_slice_in_dim(norm_gains, place * blk, blk, 1)
    pair_gains = jnp.where(
        lax.rem(lax.div(index, NEAR), 2) == 0, pair_gains, pair_gains[::-1]
    )[:, :, None]
    up = adapter_b[0].T

    a_spread = trade(down, NEAR, spread)
    a_turn = trade(down, NEAR, turned)
    b_spread = trade(up, FAR, spread)
    b_turn = trade(up, FAR, turned)
    down_pair = (jnp.stack([a_turn, a_spread]).astype(F32) * pair_gains).astype(BF16)
    up_pair = jnp.stack([b_turn, b_spread])
    up_parts = gather_up(up_pair)
    down_parts = gather_down(down_pair)
    e_half, c_half, norm = call(
        half_kernel,
        (embeds, cotangent),
        [((rows, cols), BF16), ((rows, cols), BF16), ((rows, 1), F32)],
    )
    up_pay, b_all = call(
        up_kernel,
        (e_half, c_half, *up_parts),
        [
            ((3 * rows + 2 * rank, rank), BF16),
            ((2, 8, half, rank), BF16),
        ],
    )
    up_other = cross(up_pay, 0)
    down_pay, a_all = call(
        down_kernel,
        (e_half, b_all, *down_parts),
        [((2 * rows + rank, rank), BF16), ((4, 4, blk, rank), BF16)],
    )
    down_other = cross(down_pay, 0)
    hkeep, hsend, akeep, asend, back, vees, coef = call(
        rows_kernel,
        (e_half, c_half, up_pay, up_other, down_pay, down_other, norm, a_all, b_all),
        [
            ((2, 2, 2, half, rank), BF16), ((2, 2, 2, half, rank), BF16),
            ((2, 2, 2, blk, rank), BF16), ((2, 2, 2, blk, rank), BF16),
            ((rows, cols), BF16), ((2, rows, rank), BF16), ((rows, rank), F32),
        ],
        [pltpu.VMEM((4, 4, blk, rank), BF16), pltpu.VMEM((2, 8, half, rank), BF16)],
        24,
    )

    recv = swap(hsend, CORE)
    h_side = add(hkeep[1], recv[1])
    h_mine = add(hkeep[0], recv[0])
    recv = swap(asend, CORE)
    g_far_side = add(akeep[1, 1], recv[1, 1])
    g_side = add(akeep[1, 0], recv[1, 0])
    g_mine = add(akeep[0], recv[0])
    recv = swap(h_side, Y)
    h_near = add(h_mine[1], recv[1])
    h_mine = add(h_mine[0], recv[0])
    recv = swap(h_near, NEAR)
    h_own = add(h_mine[0], recv[0])
    h_other = add(h_mine[1], recv[1])
    h_own = add(h_own, swap(h_own, FAR))
    h_other = add(cross(h_other, FAR), cross(h_other, 0))
    grad_b_parts = gather_up(jnp.stack([h_own, h_other]))

    far = add(g_mine[1], swap(g_far_side, Y))
    near = (g_mine[0], swap(g_side, Y))
    tall = ((blk + 16, rank), BF16)
    turn_out, join_out = call(last_kernel, (*near, swap(far, FAR), a_all), [tall, tall])
    grad_a, grad_gain = call(
        grad_a_kernel,
        (trade(turn_out, NEAR, turned), trade(join_out, NEAR, joined), gain, gains),
        [((blk, rank), F32), ((2, blk), F32)],
    )
    (embed_cols,) = call(embed_kernel, (e_half, back, vees, coef, a_all), [((rows, cols), BF16)])
    (grad_b,) = call(
        grad_b_kernel, grad_b_parts, [((rank, width), F32)], [pltpu.VMEM((16, half, rank), BF16)]
    )
    return (grad_a[None], grad_b[None], grad_gain, embed_cols)


def general(embeds, cotangent, adapter_a, adapter_b, norm_gains):
    sections = lax.axis_size("section")
    section = lax.axis_index("section")
    index = lax.axis_index("dp")
    _, width = embeds.shape
    cols = width // sections
    down = adapter_a[0]
    blk, rank = down.shape
    gain_row = lax.dynamic_index_in_dim(norm_gains, section % 2, 0, keepdims=False)
    gain = lax.dynamic_slice_in_dim(gain_row, index * blk, blk, 0)[:, None]
    scaled = (down.astype(F32) * gain).astype(BF16)
    down_all = lax.all_gather(lax.all_gather(scaled, "dp", axis=0, tiled=True), "section")
    up_all = lax.all_gather(lax.all_gather(adapter_b[0].T, "dp", axis=0, tiled=True), "section")
    start = section * cols
    tops = lax.dynamic_slice_in_dim(down_all, start, cols, 1)
    bottoms = lax.dynamic_slice_in_dim(down_all, width + start, cols, 1)
    ups = lax.dynamic_slice_in_dim(up_all, start, cols, 1)
    e = lax.dynamic_slice_in_dim(embeds, start, cols, 1)
    c = lax.dynamic_slice_in_dim(cotangent, start, cols, 1)
    norm = jnp.sum(jnp.square(embeds.astype(F32)), axis=1, keepdims=True)

    def project(left, right):
        return lax.dot_general(right, left, (((1,), (1,)), ((), ())), preferred_element_type=F32)

    def pairs(left, right):
        return jnp.einsum("tcr,ucq->turq", left, right, preferred_element_type=F32)

    lows, ups_e, ups_c, mixed, square = lax.psum(
        (
            project(e, tops) + project(e, bottoms),
            project(e, ups),
            project(c, ups),
            pairs(ups, tops),
            pairs(ups, ups),
        ),
        "section",
    )
    lows, ups_e, ups_c = (jnp.swapaxes(value, 1, 2) for value in (lows, ups_e, ups_c))
    scale = 1.0 / (2 * width)

    def exact(left, right):
        return jnp.dot(left, right, precision=lax.Precision.HIGHEST)

    reds, invs, spans = [], [], []
    for s in range(sections):
        full = 2.0 * norm
        low = lows[s]
        for t in range(s):
            red = reds[t].astype(F32)
            low = low + exact(red, mixed[t, s])
            full = full + jnp.sum(red * (2.0 * ups_e[t]), axis=1, keepdims=True)
            for q in range(s):
                other = exact(reds[q].astype(F32), square[q, t])
                full = full + jnp.sum(red * other, axis=1, keepdims=True)
        inv = lax.rsqrt(jnp.maximum(full, norm) * scale + epsilon)
        invs.append(inv)
        spans.append(inv * low)
        reds.append((inv * low).astype(BF16))
    vees, coefs = [None] * sections, [None] * sections
    for s in reversed(range(sections)):
        grad = ups_c[s]
        for t in range(s + 1, sections):
            hidden = ups_e[s]
            for q in range(t):
                hidden = hidden + exact(reds[q].astype(F32), square[q, s])
            grad = grad + exact(vees[t].astype(F32), mixed[s, t].T) - coefs[t] * hidden
        mean = jnp.sum(grad * spans[s], axis=1, keepdims=True) * scale
        coefs[s] = invs[s] * invs[s] * mean
        vees[s] = (invs[s] * grad).astype(BF16)
    hiddens = [e.astype(F32)]
    for s in range(sections - 1):
        hiddens.append(hiddens[s] + dot(reds[s], ups[s], 1, 1))
    back = c.astype(F32)
    embed_cols = jnp.zeros_like(back)
    terms = [None] * sections
    for s in reversed(range(sections)):
        h = hiddens[s].astype(BF16)
        terms[s] = jnp.stack(
            [
                dot(h, vees[s], 0, 0),
                dot(e, vees[s], 0, 0),
                dot(back.astype(BF16), reds[s], 0, 0),
            ]
        )
        embed_cols = embed_cols + dot(vees[s], bottoms[s], 1, 1) - coefs[s] * e.astype(F32)
        back = back + dot(vees[s], tops[s], 1, 1) - coefs[s] * hiddens[s]
    embed_cols = (embed_cols + back).astype(BF16)
    sums = lax.psum(jnp.stack(terms), "dp")
    mine = lax.all_to_all(sums, "section", 0, 2, tiled=True)[0]
    outer = lax.dynamic_slice_in_dim(mine[:2].reshape(2 * width, rank), index * blk, blk, 0)
    part = jnp.sum(outer * down.astype(F32), axis=1)
    parity = section % 2
    gain_pair = jnp.stack([jnp.where(parity == 0, part, 0.0), jnp.where(parity == 1, part, 0.0)])
    return ((gain * outer)[None], mine[2].T[None], lax.psum(gain_pair, "section"), embed_cols)


def solution(mesh):
    in_specs = (
        P("dp", None),
        P("dp", None),
        P("section", "dp", None),
        P("section", None, "dp"),
        P(),
    )
    out_specs = (
        P("section", "dp", None),
        P("section", None, None),
        P(None, "dp"),
        P("dp", "section"),
    )
    fast = mesh.shape["section"] == 2 and mesh.shape["dp"] == 16
    return jax.shard_map(
        paired if fast else general,
        mesh=mesh,
        in_specs=in_specs,
        out_specs=out_specs,
        check_vma=False,
    )
```

```python
import jax
import jax.numpy as jnp
from jax import lax
from jax.experimental import pallas as pl
from jax.experimental.pallas import tpu as pltpu
from jax.sharding import PartitionSpec as P

epsilon = 1e-05

F32 = jnp.float32
BF16 = jnp.bfloat16

CORE, Y, NEAR, FAR = 1, 2, 4, 8


def dot(left, right, left_dim=1, right_dim=0):
    return lax.dot_general(
        left, right, (((left_dim,), (right_dim,)), ((), ())), preferred_element_type=F32
    )


def swap(block, mask):
    count = lax.axis_size("dp")
    return lax.ppermute(block, "dp", [(i, i ^ mask) for i in range(count)])


def cross(block, mask):
    count = lax.axis_size("dp")
    route = [(i, (i + count) % (2 * count) ^ mask) for i in range(2 * count)]
    return lax.ppermute(block, ("section", "dp"), route)


def trade(block, mask, step):
    count = lax.axis_size("dp")
    route = []
    for section in range(2):
        for index in range(count):
            to_section, to_bit = step(section, int(bool(index & mask)))
            target = to_section * count + ((index & ~mask) | (mask if to_bit else 0))
            route.append((section * count + index, target))
    return lax.ppermute(block, ("section", "dp"), route)


def turned(s, b):
    return (b, s)


def spread(s, b):
    return (s, 1 - b) if s == b else (1 - s, b)


def joined(s, b):
    return (1 - s, b) if s == b else (s, 1 - b)


def add(left, right):
    return (left.astype(F32) + right.astype(F32)).astype(BF16)


def gather_up(pair):
    side = swap(pair, Y)
    near = swap(pair, NEAR)
    both = swap(pair, NEAR | Y)
    chips = (pair, near, side, both)
    return *chips, *(swap(block, CORE) for block in chips)


UP_MASKS = (0, NEAR, Y, NEAR | Y, CORE, CORE | NEAR, CORE | Y, CORE | NEAR | Y)


def gather_down(pair):
    far = swap(pair, FAR)
    chips = (pair, swap(pair, Y), far, swap(far, Y))
    return *chips, *(swap(block, CORE) for block in chips)


DOWN_MASKS = (0, Y, FAR, FAR | Y, CORE, CORE | Y, CORE | FAR, CORE | FAR | Y)


def pick_kernel(own_ref, other_ref, keep_ref, send_ref):
    bit = lax.rem(lax.div(lax.axis_index("dp"), FAR), 2)

    @pl.when(bit == lax.axis_index("section"))
    def _():
        keep_ref[...] = own_ref[...]
        send_ref[...] = other_ref[...]

    @pl.when(bit != lax.axis_index("section"))
    def _():
        keep_ref[...] = other_ref[...]
        send_ref[...] = own_ref[...]


def half_kernel(e_all, c_all, e_ref, c_ref, norm_ref):
    half = e_ref.shape[1]
    columns = pl.ds(pl.multiple_of(lax.axis_index("section") * half, 128), half)
    e_ref[...] = e_all[:, columns]
    c_ref[...] = c_all[:, columns]
    norm_ref[...] = jnp.sum(jnp.square(e_all[...].astype(F32)), axis=1, keepdims=True)


def up_kernel(e_ref, c_ref, *refs):
    *blocks, pay_ref, b_ref = refs
    section, index = lax.axis_index("section"), lax.axis_index("dp")
    for block, mask in zip(blocks, UP_MASKS):
        place = lax.rem(jnp.bitwise_xor(index, mask), 8)
        for j in range(2):
            b_ref[jnp.bitwise_xor(section, j), place] = block[j]
    cols = b_ref.shape[1] * b_ref.shape[2]
    rank = b_ref.shape[3]
    rows = e_ref.shape[0]
    b0, b1 = (b_ref[k].reshape(cols, rank) for k in range(2))
    square = dot(b0, b0, 0, 0)
    e = e_ref[...]
    c = c_ref[...]
    both = dot(c, jnp.concatenate([b0, b1], axis=1)).astype(BF16)
    pay_ref[pl.ds(0, rows), :] = dot(e, b0).astype(BF16)
    pay_ref[pl.ds(rows, rows), :] = both[:, :rank]
    pay_ref[pl.ds(2 * rows, rows), :] = both[:, rank:]
    high = square.astype(BF16)
    pay_ref[pl.ds(3 * rows, rank), :] = high
    pay_ref[pl.ds(3 * rows + rank, rank), :] = (square - high.astype(F32)).astype(BF16)


def down_kernel(e_ref, b_ref, *refs):
    *blocks, pay_ref, a_ref = refs
    index = lax.axis_index("dp")
    bit = lax.rem(lax.div(index, NEAR), 2)
    for block, mask in zip(blocks, DOWN_MASKS):
        holder = jnp.bitwise_xor(index, mask)
        for j in range(2):
            panel = 2 * lax.div(holder, FAR) + jnp.bitwise_xor(bit, j)
            a_ref[panel, lax.rem(holder, 4)] = block[j]
    cols = a_ref.shape[1] * a_ref.shape[2]
    rank = a_ref.shape[3]
    rows = e_ref.shape[0]
    p0, p1, q0, q1 = (a_ref[k].reshape(cols, rank) for k in range(4))
    w0 = (p0.astype(F32) + q0.astype(F32)).astype(BF16)
    w1 = (p1.astype(F32) + q1.astype(F32)).astype(BF16)
    e = e_ref[...]
    both = dot(e, jnp.concatenate([w0, w1], axis=1)).astype(BF16)
    pay_ref[pl.ds(0, rows), :] = both[:, :rank]
    pay_ref[pl.ds(rows, rows), :] = both[:, rank:]
    b0 = b_ref[0].reshape(cols, rank)
    pay_ref[pl.ds(2 * rows, rank), :] = dot(b0, p1, 0, 0).astype(BF16)


def rows_kernel(
    e_ref, c_ref, up_mine, up_other, down_mine, down_other, norm_ref, a_ref, b_ref,
    hkeep_ref, hsend_ref, akeep_ref, asend_ref, back_ref, v_ref, coef_ref, apan, hpan,
):
    section, index = lax.axis_index("section"), lax.axis_index("dp")
    rows, cols = e_ref.shape
    width = 2 * cols
    blk, rank = a_ref.shape[2:]

    def total(mine, other, start, size):
        part = pl.ds(start, size)
        return mine[part, :].astype(F32) + other[part, :].astype(F32)

    e0, y0, y1 = (total(up_mine, up_other, k * rows, rows) for k in range(3))
    square = total(up_mine, up_other, 3 * rows, rank)
    square = square + total(up_mine, up_other, 3 * rows + rank, rank)
    a0, a1 = (total(down_mine, down_other, k * rows, rows) for k in range(2))
    mixed = total(down_mine, down_other, 2 * rows, rank).astype(BF16)
    high = square.astype(BF16)
    low = (square - high.astype(F32)).astype(BF16)
    norm = norm_ref[...]
    scale = 1.0 / (2 * width)

    inv0 = lax.rsqrt(2.0 * norm * scale + epsilon)
    r0 = (inv0 * a0).astype(BF16)
    r0f = r0.astype(F32)
    r0s = dot(r0, high) + dot(r0, low)
    full = 2.0 * norm + jnp.sum(r0f * (2.0 * e0 + r0s), axis=1, keepdims=True)
    inv1 = lax.rsqrt(jnp.maximum(full, norm) * scale + epsilon)
    r1f = inv1 * (a1 + dot(r0, mixed))
    r1 = r1f.astype(BF16)
    m1 = jnp.sum(y1 * r1f, axis=1, keepdims=True) * scale
    c1 = inv1 * inv1 * m1
    v1 = (inv1 * y1).astype(BF16)
    u0 = y0 + dot(v1, mixed, 1, 1) - c1 * (e0 + r0s)
    m0 = jnp.sum(u0 * r0f, axis=1, keepdims=True) * scale
    c0 = inv0 * inv0 * m0
    v0 = (inv0 * u0).astype(BF16)

    e = e_ref[...]
    c = c_ref[...]
    b0 = b_ref[0].reshape(cols, rank)
    p1 = a_ref[1].reshape(cols, rank)
    h1f = e.astype(F32) + dot(r0, b0, 1, 1)
    backf = c.astype(F32) + dot(v1, p1, 1, 1) - c1 * h1f
    h1 = h1f.astype(BF16)
    back = backf.astype(BF16)
    back_ref[...] = back
    v_ref[0] = v0
    v_ref[1] = v1
    coef_ref[...] = jnp.broadcast_to(2.0 * c0 + c1, coef_ref.shape)

    hpan[0] = dot(back, r0, 0, 0).astype(BF16).reshape(8, blk // 2, rank)
    hpan[1] = dot(c, r1, 0, 0).astype(BF16).reshape(8, blk // 2, rank)
    both = dot(e, jnp.concatenate([v0, v1], axis=1), 0, 0).astype(BF16)
    g0 = both[:, :rank].reshape(4, blk, rank)
    apan[0] = g0
    apan[2] = g0
    apan[1] = dot(h1, v1, 0, 0).astype(BF16).reshape(4, blk, rank)
    apan[3] = both[:, rank:].reshape(4, blk, rank)

    bit = lax.rem(lax.div(index, NEAR), 2)
    for core, out in enumerate((hkeep_ref, hsend_ref)):
        for y in range(2):
            for near in range(2):
                place = lax.rem(jnp.bitwise_xor(index, core * CORE + y * Y + near * NEAR), 8)
                for j in range(2):
                    out[y, near, j] = hpan[jnp.bitwise_xor(section, j), place]
    for core, out in enumerate((akeep_ref, asend_ref)):
        for y in range(2):
            for far in range(2):
                holder = jnp.bitwise_xor(index, core * CORE + y * Y + far * FAR)
                for j in range(2):
                    panel = 2 * lax.div(holder, FAR) + jnp.bitwise_xor(bit, j)
                    out[y, far, j] = apan[panel, lax.rem(holder, 4)]


def embed_kernel(e_ref, back_ref, v_ref, coef_ref, a_ref, out_ref):
    _, cols = back_ref.shape
    rank = a_ref.shape[3]
    w0 = (a_ref[0].astype(F32) + a_ref[2].astype(F32)).astype(BF16).reshape(cols, rank)
    q1 = a_ref[3].reshape(cols, rank)
    e = e_ref[...]
    out_ref[...] = (
        back_ref[...].astype(F32)
        + dot(v_ref[0], w0, 1, 1)
        + dot(v_ref[1], q1, 1, 1)
        - coef_ref[:, 0:1] * e.astype(F32)
    ).astype(BF16)


def grad_b_kernel(*refs):
    *parts, out_ref, natural = refs
    section, index = lax.axis_index("section"), lax.axis_index("dp")
    for part, mask in zip(parts, UP_MASKS):
        place = lax.rem(jnp.bitwise_xor(index, mask), 8)
        for j in range(2):
            natural[8 * jnp.bitwise_xor(section, j) + place] = part[j]
    blocks, size, rank = natural.shape
    out_ref[...] = natural[...].reshape(blocks * size, rank).astype(F32).T


def last_kernel(near_ref, side_ref, far_ref, a_ref, out0_ref, out1_ref):
    index = lax.axis_index("dp")
    bit = lax.rem(lax.div(index, NEAR), 2)
    blk, rank = a_ref.shape[2:]
    spare = -blk % rank
    row = lax.broadcasted_iota(jnp.int32, (out0_ref.shape[0] - blk, rank), 0)
    tail = jnp.zeros(row.shape, F32)
    ones = jnp.ones((8, rank), F32)
    chunks = (blk + spare) // rank
    for k, out in enumerate((out0_ref, out1_ref)):
        call_id = jnp.bitwise_xor(bit, k)
        mine = near_ref[k].astype(F32) + side_ref[k].astype(F32) + far_ref[k].astype(F32)
        out[pl.ds(0, blk), :] = mine.astype(BF16)
        terms = mine * a_ref[2 * lax.div(index, FAR) + call_id, lax.rem(index, 4)].astype(F32)
        terms = jnp.concatenate([terms, jnp.zeros((spare, rank), F32)])
        sums = lax.dot_general(
            ones, terms, (((1,), (1,)), ((), ())),
            precision=lax.Precision.HIGHEST, preferred_element_type=F32,
        )
        for i in range(chunks):
            piece = jnp.broadcast_to(sums[0:1, i * rank : (i + 1) * rank], row.shape)
            tail = jnp.where(row == call_id * chunks + i, piece, tail)
    for out in (out0_ref, out1_ref):
        out[pl.ds(blk, tail.shape[0]), :] = tail.astype(BF16)


def grad_a_kernel(first_ref, second_ref, column_ref, gains_ref, out_ref, gain_ref):
    blk, rank = out_ref.shape
    total = first_ref[...].astype(F32) + second_ref[...].astype(F32)
    out_ref[...] = column_ref[...] * total[:blk]
    chunks = pl.cdiv(blk, rank)
    for k in range(2):
        for i in range(chunks):
            size = min(rank, blk - i * rank)
            part = pl.ds(i * rank, size)
            line = total[blk + k * chunks + i : blk + k * chunks + i + 1, :size]
            gain_ref[pl.ds(k, 1), part] = line / gains_ref[pl.ds(k, 1), part]


VMEM = pl.BlockSpec(memory_space=pltpu.VMEM)


def call(kernel, operands, outs, scratch=(), limit=16):
    return pl.pallas_call(
        kernel,
        out_shape=[jax.ShapeDtypeStruct(shape, dtype) for shape, dtype in outs],
        in_specs=[VMEM] * len(operands),
        out_specs=[VMEM] * len(outs),
        scratch_shapes=list(scratch),
        compiler_params=pltpu.CompilerParams(vmem_limit_bytes=limit * 1024 * 1024),
    )(*operands)


def paired(embeds, cotangent, adapter_a, adapter_b, norm_gains):
    return paired_body(embeds, cotangent, adapter_a, adapter_b, norm_gains)


def paired_body(embeds, cotangent, adapter_a, adapter_b, norm_gains):
    section = lax.axis_index("section")
    index = lax.axis_index("dp")
    rows, width = embeds.shape
    cols = width // 2
    down = adapter_a[0]
    blk, rank = down.shape
    half = blk // 2
    gains = lax.dynamic_slice_in_dim(norm_gains, index * blk, blk, 1)
    gain = jnp.where(section == 0, gains[0], gains[1])[:, None]
    place = index - lax.rem(lax.div(index, NEAR), 2) * NEAR + section * NEAR
    pair_gains = lax.dynamic_slice_in_dim(norm_gains, place * blk, blk, 1)
    pair_gains = jnp.where(
        lax.rem(lax.div(index, NEAR), 2) == 0, pair_gains, pair_gains[::-1]
    )[:, :, None]
    up = adapter_b[0].T

    a_spread = trade(down, NEAR, spread)
    a_turn = trade(down, NEAR, turned)
    b_keep, b_send = call(pick_kernel, (up, swap(up, FAR)), [((half, rank), BF16)] * 2)
    b_cross = cross(b_send, 0)
    down_pair = (jnp.stack([a_turn, a_spread]).astype(F32) * pair_gains).astype(BF16)
    up_pair = jnp.stack([b_keep, b_cross])
    up_parts = gather_up(up_pair)
    down_parts = gather_down(down_pair)
    e_half, c_half, norm = call(
        half_kernel,
        (embeds, cotangent),
        [((rows, cols), BF16), ((rows, cols), BF16), ((rows, 1), F32)],
    )
    up_pay, b_all = call(
        up_kernel,
        (e_half, c_half, *up_parts),
        [
            ((3 * rows + 2 * rank, rank), BF16),
            ((2, 8, half, rank), BF16),
        ],
    )
    up_other = cross(up_pay, 0)
    down_pay, a_all = call(
        down_kernel,
        (e_half, b_all, *down_parts),
        [((2 * rows + rank, rank), BF16), ((4, 4, blk, rank), BF16)],
    )
    down_other = cross(down_pay, 0)
    hkeep, hsend, akeep, asend, back, vees, coef = call(
        rows_kernel,
        (e_half, c_half, up_pay, up_other, down_pay, down_other, norm, a_all, b_all),
        [
            ((2, 2, 2, half, rank), BF16), ((2, 2, 2, half, rank), BF16),
            ((2, 2, 2, blk, rank), BF16), ((2, 2, 2, blk, rank), BF16),
            ((rows, cols), BF16), ((2, rows, rank), BF16), ((rows, rank), F32),
        ],
        [pltpu.VMEM((4, 4, blk, rank), BF16), pltpu.VMEM((2, 8, half, rank), BF16)],
        24,
    )

    recv = swap(hsend, CORE)
    h_side = add(hkeep[1], recv[1])
    h_mine = add(hkeep[0], recv[0])
    recv = swap(asend, CORE)
    g_far_side = add(akeep[1, 1], recv[1, 1])
    g_side = add(akeep[1, 0], recv[1, 0])
    g_mine = add(akeep[0], recv[0])
    recv = swap(h_side, Y)
    h_near = add(h_mine[1], recv[1])
    h_mine = add(h_mine[0], recv[0])
    recv = swap(h_near, NEAR)
    h_own = add(h_mine[0], recv[0])
    h_other = add(h_mine[1], recv[1])
    h_own = add(h_own, swap(h_own, FAR))
    h_other = add(cross(h_other, FAR), cross(h_other, 0))
    grad_b_parts = gather_up(jnp.stack([h_own, h_other]))

    far = add(g_mine[1], swap(g_far_side, Y))
    near = (g_mine[0], swap(g_side, Y))
    tall = ((blk + 16, rank), BF16)
    turn_out, join_out = call(last_kernel, (*near, swap(far, FAR), a_all), [tall, tall])
    grad_a, grad_gain = call(
        grad_a_kernel,
        (trade(turn_out, NEAR, turned), trade(join_out, NEAR, joined), gain, gains),
        [((blk, rank), F32), ((2, blk), F32)],
    )
    (embed_cols,) = call(embed_kernel, (e_half, back, vees, coef, a_all), [((rows, cols), BF16)])
    (grad_b,) = call(
        grad_b_kernel, grad_b_parts, [((rank, width), F32)], [pltpu.VMEM((16, half, rank), BF16)]
    )
    return (grad_a[None], grad_b[None], grad_gain, embed_cols)


def general(embeds, cotangent, adapter_a, adapter_b, norm_gains):
    sections = lax.axis_size("section")
    section = lax.axis_index("section")
    index = lax.axis_index("dp")
    _, width = embeds.shape
    cols = width // sections
    down = adapter_a[0]
    blk, rank = down.shape
    gain_row = lax.dynamic_index_in_dim(norm_gains, section % 2, 0, keepdims=False)
    gain = lax.dynamic_slice_in_dim(gain_row, index * blk, blk, 0)[:, None]
    scaled = (down.astype(F32) * gain).astype(BF16)
    down_all = lax.all_gather(lax.all_gather(scaled, "dp", axis=0, tiled=True), "section")
    up_all = lax.all_gather(lax.all_gather(adapter_b[0].T, "dp", axis=0, tiled=True), "section")
    start = section * cols
    tops = lax.dynamic_slice_in_dim(down_all, start, cols, 1)
    bottoms = lax.dynamic_slice_in_dim(down_all, width + start, cols, 1)
    ups = lax.dynamic_slice_in_dim(up_all, start, cols, 1)
    e = lax.dynamic_slice_in_dim(embeds, start, cols, 1)
    c = lax.dynamic_slice_in_dim(cotangent, start, cols, 1)
    norm = jnp.sum(jnp.square(embeds.astype(F32)), axis=1, keepdims=True)

    def project(left, right):
        return lax.dot_general(right, left, (((1,), (1,)), ((), ())), preferred_element_type=F32)

    def pairs(left, right):
        return jnp.einsum("tcr,ucq->turq", left, right, preferred_element_type=F32)

    lows, ups_e, ups_c, mixed, square = lax.psum(
        (
            project(e, tops) + project(e, bottoms),
            project(e, ups),
            project(c, ups),
            pairs(ups, tops),
            pairs(ups, ups),
        ),
        "section",
    )
    lows, ups_e, ups_c = (jnp.swapaxes(value, 1, 2) for value in (lows, ups_e, ups_c))
    scale = 1.0 / (2 * width)

    def exact(left, right):
        return jnp.dot(left, right, precision=lax.Precision.HIGHEST)

    reds, invs, spans = [], [], []
    for s in range(sections):
        full = 2.0 * norm
        low = lows[s]
        for t in range(s):
            red = reds[t].astype(F32)
            low = low + exact(red, mixed[t, s])
            full = full + jnp.sum(red * (2.0 * ups_e[t]), axis=1, keepdims=True)
            for q in range(s):
                other = exact(reds[q].astype(F32), square[q, t])
                full = full + jnp.sum(red * other, axis=1, keepdims=True)
        inv = lax.rsqrt(jnp.maximum(full, norm) * scale + epsilon)
        invs.append(inv)
        spans.append(inv * low)
        reds.append((inv * low).astype(BF16))
    vees, coefs = [None] * sections, [None] * sections
    for s in reversed(range(sections)):
        grad = ups_c[s]
        for t in range(s + 1, sections):
            hidden = ups_e[s]
            for q in range(t):
                hidden = hidden + exact(reds[q].astype(F32), square[q, s])
            grad = grad + exact(vees[t].astype(F32), mixed[s, t].T) - coefs[t] * hidden
        mean = jnp.sum(grad * spans[s], axis=1, keepdims=True) * scale
        coefs[s] = invs[s] * invs[s] * mean
        vees[s] = (invs[s] * grad).astype(BF16)
    hiddens = [e.astype(F32)]
    for s in range(sections - 1):
        hiddens.append(hiddens[s] + dot(reds[s], ups[s], 1, 1))
    back = c.astype(F32)
    embed_cols = jnp.zeros_like(back)
    terms = [None] * sections
    for s in reversed(range(sections)):
        h = hiddens[s].astype(BF16)
        terms[s] = jnp.stack(
            [
                dot(h, vees[s], 0, 0),
                dot(e, vees[s], 0, 0),
                dot(back.astype(BF16), reds[s], 0, 0),
            ]
        )
        embed_cols = embed_cols + dot(vees[s], bottoms[s], 1, 1) - coefs[s] * e.astype(F32)
        back = back + dot(vees[s], tops[s], 1, 1) - coefs[s] * hiddens[s]
    embed_cols = (embed_cols + back).astype(BF16)
    sums = lax.psum(jnp.stack(terms), "dp")
    mine = lax.all_to_all(sums, "section", 0, 2, tiled=True)[0]
    outer = lax.dynamic_slice_in_dim(mine[:2].reshape(2 * width, rank), index * blk, blk, 0)
    part = jnp.sum(outer * down.astype(F32), axis=1)
    parity = section % 2
    gain_pair = jnp.stack([jnp.where(parity == 0, part, 0.0), jnp.where(parity == 1, part, 0.0)])
    return ((gain * outer)[None], mine[2].T[None], lax.psum(gain_pair, "section"), embed_cols)


def solution(mesh):
    in_specs = (
        P("dp", None),
        P("dp", None),
        P("section", "dp", None),
        P("section", None, "dp"),
        P(),
    )
    out_specs = (
        P("section", "dp", None),
        P("section", None, None),
        P(None, "dp"),
        P("dp", "section"),
    )
    fast = mesh.shape["section"] == 2 and mesh.shape["dp"] == 16
    return jax.shard_map(
        paired if fast else general,
        mesh=mesh,
        in_specs=in_specs,
        out_specs=out_specs,
        check_vma=False,
    )
```

```python
import jax
import jax.numpy as jnp
from jax import lax
from jax.experimental import pallas as pl
from jax.experimental.pallas import tpu as pltpu
from jax.sharding import PartitionSpec as P

epsilon = 1e-05

F32 = jnp.float32
BF16 = jnp.bfloat16

CORE, Y, NEAR, FAR = 1, 2, 4, 8


def dot(left, right, left_dim=1, right_dim=0):
    return lax.dot_general(
        left, right, (((left_dim,), (right_dim,)), ((), ())), preferred_element_type=F32
    )


def swap(block, mask):
    count = lax.axis_size("dp")
    return lax.ppermute(block, "dp", [(i, i ^ mask) for i in range(count)])


def cross(block, mask):
    count = lax.axis_size("dp")
    route = [(i, (i + count) % (2 * count) ^ mask) for i in range(2 * count)]
    return lax.ppermute(block, ("section", "dp"), route)


def trade(block, mask, step):
    count = lax.axis_size("dp")
    route = []
    for section in range(2):
        for index in range(count):
            to_section, to_bit = step(section, int(bool(index & mask)))
            target = to_section * count + ((index & ~mask) | (mask if to_bit else 0))
            route.append((section * count + index, target))
    return lax.ppermute(block, ("section", "dp"), route)


def turned(s, b):
    return (b, s)


def spread(s, b):
    return (s, 1 - b) if s == b else (1 - s, b)


def joined(s, b):
    return (1 - s, b) if s == b else (s, 1 - b)


def add(left, right):
    return (left.astype(F32) + right.astype(F32)).astype(BF16)


def gather_up(pair):
    side = swap(pair, Y)
    near = swap(pair, NEAR)
    both = swap(pair, NEAR | Y)
    chips = (pair, near, side, both)
    return *chips, *(swap(block, CORE) for block in chips)


UP_MASKS = (0, NEAR, Y, NEAR | Y, CORE, CORE | NEAR, CORE | Y, CORE | NEAR | Y)


def gather_down(pair):
    far = swap(pair, FAR)
    chips = (pair, swap(pair, Y), far, swap(far, Y))
    return *chips, *(swap(block, CORE) for block in chips)


DOWN_MASKS = (0, Y, FAR, FAR | Y, CORE, CORE | Y, CORE | FAR, CORE | FAR | Y)


def pick_kernel(own_ref, other_ref, keep_ref, send_ref):
    bit = lax.rem(lax.div(lax.axis_index("dp"), FAR), 2)

    @pl.when(bit == lax.axis_index("section"))
    def _():
        keep_ref[...] = own_ref[...]
        send_ref[...] = other_ref[...]

    @pl.when(bit != lax.axis_index("section"))
    def _():
        keep_ref[...] = other_ref[...]
        send_ref[...] = own_ref[...]


def half_kernel(e_all, c_all, e_ref, c_ref, norm_ref):
    half = e_ref.shape[1]
    columns = pl.ds(pl.multiple_of(lax.axis_index("section") * half, 128), half)
    e_ref[...] = e_all[:, columns]
    c_ref[...] = c_all[:, columns]
    norm_ref[...] = jnp.sum(jnp.square(e_all[...].astype(F32)), axis=1, keepdims=True)


def up_kernel(e_ref, c_ref, *refs):
    *blocks, pay_ref, b_ref = refs
    section, index = lax.axis_index("section"), lax.axis_index("dp")
    for block, mask in zip(blocks, UP_MASKS):
        place = lax.rem(jnp.bitwise_xor(index, mask), 8)
        for j in range(2):
            b_ref[jnp.bitwise_xor(section, j), place] = block[j]
    cols = b_ref.shape[1] * b_ref.shape[2]
    rank = b_ref.shape[3]
    rows = e_ref.shape[0]
    b0, b1 = (b_ref[k].reshape(cols, rank) for k in range(2))
    square = dot(b0, b0, 0, 0)
    e = e_ref[...]
    c = c_ref[...]
    both = dot(c, jnp.concatenate([b0, b1], axis=1)).astype(BF16)
    pay_ref[pl.ds(0, rows), :] = dot(e, b0).astype(BF16)
    pay_ref[pl.ds(rows, rows), :] = both[:, :rank]
    pay_ref[pl.ds(2 * rows, rows), :] = both[:, rank:]
    high = square.astype(BF16)
    pay_ref[pl.ds(3 * rows, rank), :] = high
    pay_ref[pl.ds(3 * rows + rank, rank), :] = (square - high.astype(F32)).astype(BF16)


def down_kernel(e_ref, b_ref, *refs):
    *blocks, pay_ref, a_ref = refs
    index = lax.axis_index("dp")
    bit = lax.rem(lax.div(index, NEAR), 2)
    for block, mask in zip(blocks, DOWN_MASKS):
        holder = jnp.bitwise_xor(index, mask)
        for j in range(2):
            panel = 2 * lax.div(holder, FAR) + jnp.bitwise_xor(bit, j)
            a_ref[panel, lax.rem(holder, 4)] = block[j]
    cols = a_ref.shape[1] * a_ref.shape[2]
    rank = a_ref.shape[3]
    rows = e_ref.shape[0]
    p0, p1, q0, q1 = (a_ref[k].reshape(cols, rank) for k in range(4))
    w0 = (p0.astype(F32) + q0.astype(F32)).astype(BF16)
    w1 = (p1.astype(F32) + q1.astype(F32)).astype(BF16)
    e = e_ref[...]
    both = dot(e, jnp.concatenate([w0, w1], axis=1)).astype(BF16)
    pay_ref[pl.ds(0, rows), :] = both[:, :rank]
    pay_ref[pl.ds(rows, rows), :] = both[:, rank:]
    b0 = b_ref[0].reshape(cols, rank)
    pay_ref[pl.ds(2 * rows, rank), :] = dot(b0, p1, 0, 0).astype(BF16)


def rows_kernel(
    e_ref, c_ref, up_mine, up_other, down_mine, down_other, norm_ref, a_ref, b_ref,
    hkeep_ref, hsend_ref, akeep_ref, asend_ref, back_ref, v_ref, coef_ref, apan, hpan,
):
    section, index = lax.axis_index("section"), lax.axis_index("dp")
    rows, cols = e_ref.shape
    width = 2 * cols
    blk, rank = a_ref.shape[2:]

    def total(mine, other, start, size):
        part = pl.ds(start, size)
        return mine[part, :].astype(F32) + other[part, :].astype(F32)

    e0, y0, y1 = (total(up_mine, up_other, k * rows, rows) for k in range(3))
    square = total(up_mine, up_other, 3 * rows, rank)
    square = square + total(up_mine, up_other, 3 * rows + rank, rank)
    a0, a1 = (total(down_mine, down_other, k * rows, rows) for k in range(2))
    mixed = total(down_mine, down_other, 2 * rows, rank).astype(BF16)
    high = square.astype(BF16)
    low = (square - high.astype(F32)).astype(BF16)
    norm = norm_ref[...]
    scale = 1.0 / (2 * width)

    inv0 = lax.rsqrt(2.0 * norm * scale + epsilon)
    r0 = (inv0 * a0).astype(BF16)
    r0f = r0.astype(F32)
    r0s = dot(r0, high) + dot(r0, low)
    full = 2.0 * norm + jnp.sum(r0f * (2.0 * e0 + r0s), axis=1, keepdims=True)
    inv1 = lax.rsqrt(jnp.maximum(full, norm) * scale + epsilon)
    r1f = inv1 * (a1 + dot(r0, mixed))
    r1 = r1f.astype(BF16)
    m1 = jnp.sum(y1 * r1f, axis=1, keepdims=True) * scale
    c1 = inv1 * inv1 * m1
    v1 = (inv1 * y1).astype(BF16)
    u0 = y0 + dot(v1, mixed, 1, 1) - c1 * (e0 + r0s)
    m0 = jnp.sum(u0 * r0f, axis=1, keepdims=True) * scale
    c0 = inv0 * inv0 * m0
    v0 = (inv0 * u0).astype(BF16)

    e = e_ref[...]
    c = c_ref[...]
    b0 = b_ref[0].reshape(cols, rank)
    p1 = a_ref[1].reshape(cols, rank)
    h1f = e.astype(F32) + dot(r0, b0, 1, 1)
    backf = c.astype(F32) + dot(v1, p1, 1, 1) - c1 * h1f
    h1 = h1f.astype(BF16)
    back = backf.astype(BF16)
    back_ref[...] = back
    v_ref[0] = v0
    v_ref[1] = v1
    coef_ref[...] = jnp.broadcast_to(2.0 * c0 + c1, coef_ref.shape)

    hpan[0] = dot(back, r0, 0, 0).astype(BF16).reshape(8, blk // 2, rank)
    hpan[1] = dot(c, r1, 0, 0).astype(BF16).reshape(8, blk // 2, rank)
    both = dot(e, jnp.concatenate([v0, v1], axis=1), 0, 0).astype(BF16)
    g0 = both[:, :rank].reshape(4, blk, rank)
    apan[0] = g0
    apan[2] = g0
    apan[1] = dot(h1, v1, 0, 0).astype(BF16).reshape(4, blk, rank)
    apan[3] = both[:, rank:].reshape(4, blk, rank)

    bit = lax.rem(lax.div(index, NEAR), 2)
    for core, out in enumerate((hkeep_ref, hsend_ref)):
        for y in range(2):
            for near in range(2):
                place = lax.rem(jnp.bitwise_xor(index, core * CORE + y * Y + near * NEAR), 8)
                for j in range(2):
                    out[y, near, j] = hpan[jnp.bitwise_xor(section, j), place]
    for core, out in enumerate((akeep_ref, asend_ref)):
        for y in range(2):
            for far in range(2):
                holder = jnp.bitwise_xor(index, core * CORE + y * Y + far * FAR)
                for j in range(2):
                    panel = 2 * lax.div(holder, FAR) + jnp.bitwise_xor(bit, j)
                    out[y, far, j] = apan[panel, lax.rem(holder, 4)]


def embed_kernel(e_ref, back_ref, v_ref, coef_ref, a_ref, out_ref):
    _, cols = back_ref.shape
    rank = a_ref.shape[3]
    w0 = (a_ref[0].astype(F32) + a_ref[2].astype(F32)).astype(BF16).reshape(cols, rank)
    q1 = a_ref[3].reshape(cols, rank)
    e = e_ref[...]
    out_ref[...] = (
        back_ref[...].astype(F32)
        + dot(v_ref[0], w0, 1, 1)
        + dot(v_ref[1], q1, 1, 1)
        - coef_ref[:, 0:1] * e.astype(F32)
    ).astype(BF16)


def grad_b_kernel(*refs):
    *parts, out_ref, natural = refs
    section, index = lax.axis_index("section"), lax.axis_index("dp")
    for part, mask in zip(parts, UP_MASKS):
        place = lax.rem(jnp.bitwise_xor(index, mask), 8)
        for j in range(2):
            natural[8 * jnp.bitwise_xor(section, j) + place] = part[j]
    blocks, size, rank = natural.shape
    out_ref[...] = natural[...].reshape(blocks * size, rank).astype(F32).T


def last_kernel(near_ref, side_ref, far_ref, a_ref, out0_ref, out1_ref):
    index = lax.axis_index("dp")
    bit = lax.rem(lax.div(index, NEAR), 2)
    blk, rank = a_ref.shape[2:]
    spare = -blk % rank
    row = lax.broadcasted_iota(jnp.int32, (out0_ref.shape[0] - blk, rank), 0)
    tail = jnp.zeros(row.shape, F32)
    ones = jnp.ones((8, rank), F32)
    chunks = (blk + spare) // rank
    for k, out in enumerate((out0_ref, out1_ref)):
        call_id = jnp.bitwise_xor(bit, k)
        mine = near_ref[k].astype(F32) + side_ref[k].astype(F32) + far_ref[k].astype(F32)
        out[pl.ds(0, blk), :] = mine.astype(BF16)
        terms = mine * a_ref[2 * lax.div(index, FAR) + call_id, lax.rem(index, 4)].astype(F32)
        terms = jnp.concatenate([terms, jnp.zeros((spare, rank), F32)])
        sums = lax.dot_general(
            ones, terms, (((1,), (1,)), ((), ())),
            precision=lax.Precision.HIGHEST, preferred_element_type=F32,
        )
        for i in range(chunks):
            piece = jnp.broadcast_to(sums[0:1, i * rank : (i + 1) * rank], row.shape)
            tail = jnp.where(row == call_id * chunks + i, piece, tail)
    for out in (out0_ref, out1_ref):
        out[pl.ds(blk, tail.shape[0]), :] = tail.astype(BF16)


def grad_a_kernel(first_ref, second_ref, column_ref, gains_ref, out_ref, gain_ref):
    blk, rank = out_ref.shape
    total = first_ref[...].astype(F32) + second_ref[...].astype(F32)
    out_ref[...] = column_ref[...] * total[:blk]
    chunks = pl.cdiv(blk, rank)
    for k in range(2):
        for i in range(chunks):
            size = min(rank, blk - i * rank)
            part = pl.ds(i * rank, size)
            line = total[blk + k * chunks + i : blk + k * chunks + i + 1, :size]
            gain_ref[pl.ds(k, 1), part] = line / gains_ref[pl.ds(k, 1), part]


VMEM = pl.BlockSpec(memory_space=pltpu.VMEM)


def call(kernel, operands, outs, scratch=(), limit=16):
    return pl.pallas_call(
        kernel,
        out_shape=[jax.ShapeDtypeStruct(shape, dtype) for shape, dtype in outs],
        in_specs=[VMEM] * len(operands),
        out_specs=[VMEM] * len(outs),
        scratch_shapes=list(scratch),
        compiler_params=pltpu.CompilerParams(vmem_limit_bytes=limit * 1024 * 1024),
    )(*operands)


def paired(embeds, cotangent, adapter_a, adapter_b, norm_gains):
    return paired_body(embeds, cotangent, adapter_a, adapter_b, norm_gains)


def paired_body(embeds, cotangent, adapter_a, adapter_b, norm_gains):
    section = lax.axis_index("section")
    index = lax.axis_index("dp")
    rows, width = embeds.shape
    cols = width // 2
    down = adapter_a[0]
    blk, rank = down.shape
    half = blk // 2
    gains = lax.dynamic_slice_in_dim(norm_gains, index * blk, blk, 1)
    gain = jnp.where(section == 0, gains[0], gains[1])[:, None]
    place = index - lax.rem(lax.div(index, NEAR), 2) * NEAR + section * NEAR
    pair_gains = lax.dynamic_slice_in_dim(norm_gains, place * blk, blk, 1)
    pair_gains = jnp.where(
        lax.rem(lax.div(index, NEAR), 2) == 0, pair_gains, pair_gains[::-1]
    )[:, :, None]
    up = adapter_b[0].T

    a_spread = trade(down, NEAR, spread)
    a_turn = trade(down, NEAR, turned)
    b_keep, b_send = call(pick_kernel, (up, swap(up, FAR)), [((half, rank), BF16)] * 2)
    b_cross = cross(b_send, 0)
    down_pair = (jnp.stack([a_turn, a_spread]).astype(F32) * pair_gains).astype(BF16)
    up_pair = jnp.stack([b_keep, b_cross])
    up_parts = gather_up(up_pair)
    down_parts = gather_down(down_pair)
    e_half, c_half, norm = call(
        half_kernel,
        (embeds, cotangent),
        [((rows, cols), BF16), ((rows, cols), BF16), ((rows, 1), F32)],
    )
    up_pay, b_all = call(
        up_kernel,
        (e_half, c_half, *up_parts),
        [
            ((3 * rows + 2 * rank, rank), BF16),
            ((2, 8, half, rank), BF16),
        ],
    )
    up_other = cross(up_pay, 0)
    down_pay, a_all = call(
        down_kernel,
        (e_half, b_all, *down_parts),
        [((2 * rows + rank, rank), BF16), ((4, 4, blk, rank), BF16)],
    )
    down_other = cross(down_pay, 0)
    hkeep, hsend, akeep, asend, back, vees, coef = call(
        rows_kernel,
        (e_half, c_half, up_pay, up_other, down_pay, down_other, norm, a_all, b_all),
        [
            ((2, 2, 2, half, rank), BF16), ((2, 2, 2, half, rank), BF16),
            ((2, 2, 2, blk, rank), BF16), ((2, 2, 2, blk, rank), BF16),
            ((rows, cols), BF16), ((2, rows, rank), BF16), ((rows, rank), F32),
        ],
        [pltpu.VMEM((4, 4, blk, rank), BF16), pltpu.VMEM((2, 8, half, rank), BF16)],
        24,
    )

    recv = swap(hsend, CORE)
    h_side = add(hkeep[1], recv[1])
    h_mine = add(hkeep[0], recv[0])
    recv = swap(asend, CORE)
    g_far_side = add(akeep[1, 1], recv[1, 1])
    g_side = add(akeep[1, 0], recv[1, 0])
    g_mine = add(akeep[0], recv[0])
    recv = swap(h_side, Y)
    h_near = add(h_mine[1], recv[1])
    h_mine = add(h_mine[0], recv[0])
    h_mine = add(h_mine, swap(h_near, NEAR))
    h_mine = add(h_mine, swap(h_mine, FAR))
    h_cross = cross(h_mine[1], 0)
    grad_b_parts = gather_up(jnp.stack([h_mine[0], h_cross]))

    far = add(g_mine[1], swap(g_far_side, Y))
    near = (g_mine[0], swap(g_side, Y))
    tall = ((blk + 16, rank), BF16)
    turn_out, join_out = call(last_kernel, (*near, swap(far, FAR), a_all), [tall, tall])
    grad_a, grad_gain = call(
        grad_a_kernel,
        (trade(turn_out, NEAR, turned), trade(join_out, NEAR, joined), gain, gains),
        [((blk, rank), F32), ((2, blk), F32)],
    )
    (embed_cols,) = call(embed_kernel, (e_half, back, vees, coef, a_all), [((rows, cols), BF16)])
    (grad_b,) = call(
        grad_b_kernel, grad_b_parts, [((rank, width), F32)], [pltpu.VMEM((16, half, rank), BF16)]
    )
    return (grad_a[None], grad_b[None], grad_gain, embed_cols)


def general(embeds, cotangent, adapter_a, adapter_b, norm_gains):
    sections = lax.axis_size("section")
    section = lax.axis_index("section")
    index = lax.axis_index("dp")
    _, width = embeds.shape
    cols = width // sections
    down = adapter_a[0]
    blk, rank = down.shape
    gain_row = lax.dynamic_index_in_dim(norm_gains, section % 2, 0, keepdims=False)
    gain = lax.dynamic_slice_in_dim(gain_row, index * blk, blk, 0)[:, None]
    scaled = (down.astype(F32) * gain).astype(BF16)
    down_all = lax.all_gather(lax.all_gather(scaled, "dp", axis=0, tiled=True), "section")
    up_all = lax.all_gather(lax.all_gather(adapter_b[0].T, "dp", axis=0, tiled=True), "section")
    start = section * cols
    tops = lax.dynamic_slice_in_dim(down_all, start, cols, 1)
    bottoms = lax.dynamic_slice_in_dim(down_all, width + start, cols, 1)
    ups = lax.dynamic_slice_in_dim(up_all, start, cols, 1)
    e = lax.dynamic_slice_in_dim(embeds, start, cols, 1)
    c = lax.dynamic_slice_in_dim(cotangent, start, cols, 1)
    norm = jnp.sum(jnp.square(embeds.astype(F32)), axis=1, keepdims=True)

    def project(left, right):
        return lax.dot_general(right, left, (((1,), (1,)), ((), ())), preferred_element_type=F32)

    def pairs(left, right):
        return jnp.einsum("tcr,ucq->turq", left, right, preferred_element_type=F32)

    lows, ups_e, ups_c, mixed, square = lax.psum(
        (
            project(e, tops) + project(e, bottoms),
            project(e, ups),
            project(c, ups),
            pairs(ups, tops),
            pairs(ups, ups),
        ),
        "section",
    )
    lows, ups_e, ups_c = (jnp.swapaxes(value, 1, 2) for value in (lows, ups_e, ups_c))
    scale = 1.0 / (2 * width)

    def exact(left, right):
        return jnp.dot(left, right, precision=lax.Precision.HIGHEST)

    reds, invs, spans = [], [], []
    for s in range(sections):
        full = 2.0 * norm
        low = lows[s]
        for t in range(s):
            red = reds[t].astype(F32)
            low = low + exact(red, mixed[t, s])
            full = full + jnp.sum(red * (2.0 * ups_e[t]), axis=1, keepdims=True)
            for q in range(s):
                other = exact(reds[q].astype(F32), square[q, t])
                full = full + jnp.sum(red * other, axis=1, keepdims=True)
        inv = lax.rsqrt(jnp.maximum(full, norm) * scale + epsilon)
        invs.append(inv)
        spans.append(inv * low)
        reds.append((inv * low).astype(BF16))
    vees, coefs = [None] * sections, [None] * sections
    for s in reversed(range(sections)):
        grad = ups_c[s]
        for t in range(s + 1, sections):
            hidden = ups_e[s]
            for q in range(t):
                hidden = hidden + exact(reds[q].astype(F32), square[q, s])
            grad = grad + exact(vees[t].astype(F32), mixed[s, t].T) - coefs[t] * hidden
        mean = jnp.sum(grad * spans[s], axis=1, keepdims=True) * scale
        coefs[s] = invs[s] * invs[s] * mean
        vees[s] = (invs[s] * grad).astype(BF16)
    hiddens = [e.astype(F32)]
    for s in range(sections - 1):
        hiddens.append(hiddens[s] + dot(reds[s], ups[s], 1, 1))
    back = c.astype(F32)
    embed_cols = jnp.zeros_like(back)
    terms = [None] * sections
    for s in reversed(range(sections)):
        h = hiddens[s].astype(BF16)
        terms[s] = jnp.stack(
            [
                dot(h, vees[s], 0, 0),
                dot(e, vees[s], 0, 0),
                dot(back.astype(BF16), reds[s], 0, 0),
            ]
        )
        embed_cols = embed_cols + dot(vees[s], bottoms[s], 1, 1) - coefs[s] * e.astype(F32)
        back = back + dot(vees[s], tops[s], 1, 1) - coefs[s] * hiddens[s]
    embed_cols = (embed_cols + back).astype(BF16)
    sums = lax.psum(jnp.stack(terms), "dp")
    mine = lax.all_to_all(sums, "section", 0, 2, tiled=True)[0]
    outer = lax.dynamic_slice_in_dim(mine[:2].reshape(2 * width, rank), index * blk, blk, 0)
    part = jnp.sum(outer * down.astype(F32), axis=1)
    parity = section % 2
    gain_pair = jnp.stack([jnp.where(parity == 0, part, 0.0), jnp.where(parity == 1, part, 0.0)])
    return ((gain * outer)[None], mine[2].T[None], lax.psum(gain_pair, "section"), embed_cols)


def solution(mesh):
    in_specs = (
        P("dp", None),
        P("dp", None),
        P("section", "dp", None),
        P("section", None, "dp"),
        P(),
    )
    out_specs = (
        P("section", "dp", None),
        P("section", None, None),
        P(None, "dp"),
        P("dp", "section"),
    )
    fast = mesh.shape["section"] == 2 and mesh.shape["dp"] == 16
    return jax.shard_map(
        paired if fast else general,
        mesh=mesh,
        in_specs=in_specs,
        out_specs=out_specs,
        check_vma=False,
    )
```
